256 devices in a mesh: tm: 8 (over y_lo, x), tok: 32 (over y_hi, z, core).
Axes of the slice: x: 4, y: 4 (y_hi: 2, y_lo: 2; y = y_hi * 2 + y_lo), z: 8, core: 2. Of those that a mesh axis runs over, the one named last changes fastest.
Arguments:
- start: bfloat16 [4096, 1536], P('tok'), may hold values from -6 to 6
- trajectory: bfloat16 [16, 4096, 1536], P('tm', 'tok'), may hold values from -6 to 6
- plan: int32 [17], replicated, may hold values from 0 to 1000, as said below
- neighbors: int32 [64, 3], P('tok'), may hold values from 0 to 63, as said below
- mod_weight: bfloat16 [256, 3072], replicated, may hold values from -0.75 to 0.75
- w_qkv: bfloat16 [1536, 4608], P('tok'), may hold values from -0.15625 to 0.15625
- w_out: bfloat16 [1536, 1536], P('tok'), may hold values from -1.25 to 1.25
Outputs:
- updated: float32 [16, 4096, 1536], P('tm', 'tok')
The draws below stay inside these ranges and needn't reach their ends.
Inputs may be any that keep to these rules, and one draw needn't show every extreme that they name: `plan`: strictly decreasing from 1000 at the first entry to 0 at the last. `neighbors`: entry 0 of row c is c; the other entries lie within 2 of c.
All inputs are finite; a program needn't handle non-finite values.
Results may differ from the reference program's by a relative error of at most 0.0045.
Values may be sent and summed in bfloat16 or wider, within the bound.
A program may use at most 128 MiB of HBM per device.

```python
import math
import jax
import jax.numpy as jnp
from jax import lax

HEADS = 12
HEAD_DIM = 128
TEMB = 256
NSCHED = 1000
NB = 3
D = 1536
TILE = 64
TSTEPS = 16
TOKENS = 4096
NTILES = 64


def draw_plan(key, part):
    inner = jax.random.permutation(key, NSCHED - 1)[:TSTEPS - 1] + 1
    inner = -jnp.sort(-inner)
    head = jnp.full((1,), NSCHED, jnp.int32)
    tail = jnp.zeros((1,), jnp.int32)
    return jnp.concatenate([head, inner.astype(jnp.int32), tail]).astype(jnp.int32)


def draw_neighbors(key, part):
    offsets = jnp.array([-2, -1, 1, 2], jnp.int32)
    keys = jax.random.split(key, NTILES)
    picks = jax.vmap(lambda one: jax.random.permutation(one, 4))(keys)[:, :2]
    chosen = offsets[picks]
    own = jnp.arange(NTILES, dtype=jnp.int32)[:, None]
    target = own + chosen
    outside = (target < 0) | (target >= NTILES)
    target = jnp.where(outside, own - chosen, target)
    return jnp.concatenate([own, target], axis=1).astype(jnp.int32)


def block_scale(rng, shape, cuts, least, top_value):
    def one(position, shards_of):
        steps = jax.random.uniform(jax.random.fold_in(jax.random.fold_in(rng, 6), position), (shards_of,), jnp.float32, least / len(cuts), top_value / len(cuts))
        return jnp.repeat(jnp.exp(steps), shape[position] // shards_of).reshape((-1,) + (1,) * (len(shape) - position - 1))

    level = one(*cuts[0])
    for cut in cuts[1:]:
        level = level * one(*cut)
    return level


def centred(stream_key, extent, scale, most, cuts=(), kind=jnp.bfloat16):
    result = scale * jax.random.normal(stream_key, extent, jnp.float32)
    if cuts:
        result = result * block_scale(stream_key, extent, cuts, -0.22, 0.18)
    return jnp.clip(result, -most, most).astype(kind)


def setup_inputs(seed: int = 0) -> dict:
    key_of = jax.random.split(jax.random.key(seed), 8)
    start = centred(key_of[0], (TOKENS, D), 1.0, 6.0, ((0, 32),))
    trajectory = centred(key_of[1], (TSTEPS, TOKENS, D), 1.0, 6.0, ((0, 8), (1, 32)))
    plan = draw_plan(jax.random.fold_in(key_of[7], 71), 0)
    neighbors = draw_neighbors(jax.random.fold_in(key_of[7], 71), 0)
    mod_weight = centred(key_of[4], (TEMB, 2 * D), (TEMB // 4) ** -0.5, 0.75)
    w_qkv = centred(key_of[5], (D, 3 * D), D ** -0.5, 0.15625, ((0, 32),))
    w_out = centred(key_of[6], (D, D), (D // 64) ** -0.5, 1.25, ((0, 32),))
    return {"start": start, "trajectory": trajectory, "plan": plan, "neighbors": neighbors, "mod_weight": mod_weight, "w_qkv": w_qkv, "w_out": w_out}


def time_mod(times, mod_weight):
    half = TEMB // 2
    freqs = jnp.exp(-math.log(10000.0) * jnp.arange(half, dtype=jnp.float32) / half)
    angle = 1000.0 * times[:, None] * freqs[None, :]
    embed = jnp.concatenate([jnp.cos(angle), jnp.sin(angle)], axis=1)
    act = jax.nn.silu(embed).astype(jnp.bfloat16)
    return jnp.dot(act, mod_weight, preferred_element_type=jnp.float32)

def modulate(state, shift, scale):
    values = state.astype(jnp.float32)
    center = values - lax.optimization_barrier(jnp.mean(values, -1, keepdims=True))
    spread = lax.optimization_barrier(jnp.mean(center * center, -1, keepdims=True))
    return (center / jnp.sqrt(spread + 1e-06) * (1.0 + scale) + shift).astype(jnp.bfloat16)

def head_norm(values):
    return (values / jnp.sqrt(lax.optimization_barrier(jnp.mean(values * values, -1, keepdims=True)) + 1e-06)).astype(jnp.bfloat16)

def drift_one(state, shift, scale, neighbors, w_qkv, w_out):
    normed = modulate(state, shift[None, :], scale[None, :])
    qkv = jnp.dot(normed, w_qkv, preferred_element_type=jnp.float32)
    query = head_norm(qkv[:, :D].reshape(NTILES, TILE, HEADS, HEAD_DIM))
    keys = head_norm(qkv[:, D:2 * D].reshape(NTILES, TILE, HEADS, HEAD_DIM))
    values = qkv[:, 2 * D:].astype(jnp.bfloat16).reshape(NTILES, TILE, HEADS, HEAD_DIM)
    near_keys = jnp.take(keys, neighbors, axis=0).reshape(NTILES, NB * TILE, HEADS, HEAD_DIM)
    near_values = jnp.take(values, neighbors, axis=0).reshape(NTILES, NB * TILE, HEADS, HEAD_DIM)
    score = jnp.einsum('cqha,ckha->chqk', query.astype(jnp.float32), near_keys.astype(jnp.float32)) / math.sqrt(HEAD_DIM)
    expo = jnp.exp(score)
    prob = (expo / lax.optimization_barrier(jnp.sum(expo, -1, keepdims=True))).astype(jnp.bfloat16)
    attn = jnp.einsum('chqk,ckha->cqha', prob.astype(jnp.float32), near_values.astype(jnp.float32))
    attn = attn.astype(jnp.bfloat16).reshape(TOKENS, D)
    return jnp.dot(attn, w_out, preferred_element_type=jnp.float32)

def reference(start, trajectory, plan, neighbors, mod_weight, w_qkv, w_out):
    times = plan.astype(jnp.float32) / NSCHED
    steps = times[:-1] - times[1:]
    mod = time_mod(times[:TSTEPS], mod_weight)

    def single(item):
        state, shift, scale = item
        return drift_one(state, shift, scale, neighbors, w_qkv, w_out)
    drift = lax.map(single, (trajectory, mod[:, :D], mod[:, D:]))
    scaled = steps[:, None, None] * drift
    before = jnp.cumsum(scaled, axis=0) - scaled
    return start.astype(jnp.float32)[None] - before
```

```python
import functools
import math

import jax
import jax.numpy as jnp
from jax import lax
from jax.experimental import pallas as pl
from jax.experimental.pallas import tpu as pltpu
from jax.sharding import PartitionSpec as P

NSCHED = 1000
XG = 4
ZG = 8
HL = 3
HD = 128
CW = HL * HD
TILE = 64
MESH = pl.DeviceIdType.MESH


def time_mod(times, mod_weight):
    half = mod_weight.shape[0] // 2
    freqs = jnp.exp(-math.log(10000.0) * jnp.arange(half, dtype=jnp.float32) / half)
    angle = 1000.0 * times[:, None] * freqs[None, :]
    embed = jnp.concatenate([jnp.cos(angle), jnp.sin(angle)], axis=1)
    act = jax.nn.silu(embed).astype(jnp.bfloat16)
    return jnp.dot(act, mod_weight, preferred_element_type=jnp.float32)


def modulate(state, shift, scale):
    values = state.astype(jnp.float32)
    center = values - jnp.mean(values, -1, keepdims=True)
    spread = jnp.mean(center * center, -1, keepdims=True)
    return (center / jnp.sqrt(spread + 1e-06) * (1.0 + scale) + shift).astype(jnp.bfloat16)


class Ring:
    def __init__(self, buf, send, recv, pos, peers):
        self.buf, self.send, self.recv = buf, send, recv
        self.yh, self.z, self.c = pos
        self.peers = peers
        self.sent = []

    def block(self, yh, z):
        return self.buf.at[yh, z, self.c]

    def push(self, ref, i, peer):
        copy = pltpu.make_async_remote_copy(
            src_ref=ref, dst_ref=ref, send_sem=self.send.at[i], recv_sem=self.recv.at[i],
            device_id=self.peers[peer], device_id_type=MESH,
        )
        copy.start()
        self.sent.append(copy)

    def arrive(self, ref, i, peer):
        pltpu.make_async_remote_copy(
            src_ref=ref, dst_ref=ref, send_sem=self.send.at[i], recv_sem=self.recv.at[i],
            device_id=self.peers[peer], device_id_type=MESH,
        ).wait_recv()

    def own(self):
        mine = self.block(self.yh, self.z)
        self.push(mine, 0, "z+")
        self.push(mine, 4, "z-")
        self.push(mine, 7, "part")

    def step(self, s):
        low = self.block(self.yh, lax.rem(self.z + ZG - s, ZG))
        self.arrive(low, s - 1, "z+")
        if s < 4:
            self.push(low, s, "z+")
        self.push(low, 7 + s, "part")
        if s < 4:
            high = self.block(self.yh, lax.rem(self.z + s, ZG))
            self.arrive(high, 3 + s, "z-")
            if s < 3:
                self.push(high, 4 + s, "z-")
            self.push(high, 11 + s, "part")

    def share_own(self):
        self.push(self.buf.at[self.yh, :, self.c], 15, "core")

    def share_other(self):
        other = 1 - self.yh
        self.arrive(self.block(other, self.z), 7, "part")
        for s in range(1, 5):
            self.arrive(self.block(other, lax.rem(self.z + ZG - s, ZG)), 7 + s, "part")
            if s < 4:
                self.arrive(self.block(other, lax.rem(self.z + s, ZG)), 11 + s, "part")
        self.push(self.buf.at[other, :, self.c], 16, "core")

    def shared(self):
        self.arrive(self.buf.at[self.yh, :, 1 - self.c], 15, "core")
        self.arrive(self.buf.at[1 - self.yh, :, 1 - self.c], 16, "core")

    def finish(self):
        for copy in self.sent:
            copy.wait_send()


def kernel(
    h_ref, wqkv_ref, wout_ref, start_ref, nb_ref, step_ref, out_ref,
    hbuf, wbuf, wo, kv0, kv1, kv2, kv3, abuf, tsend, trecv, sbuf, sall,
    lsem, hs, hr, ws, wr, os, orecv, ks, kr, ts, tr, ss, sr,
):
    tm, tok = lax.axis_index("tm"), lax.axis_index("tok")
    x, yl = lax.rem(tm, XG), lax.div(tm, XG)
    yh, z, c = lax.div(tok, 2 * ZG), lax.div(lax.rem(tok, 2 * ZG), 2), lax.rem(tok, 2)
    width = h_ref.shape[1]
    rows = h_ref.shape[0]
    part_rows = rows // 2
    ntok = 4 * ZG

    def at_x(k):
        return {"tm": yl * XG + lax.rem(x + k, XG), "tok": tok}

    def at_tok(k):
        return {"tm": tm, "tok": lax.rem(tok + ntok + k, ntok)}

    peers = {
        "z+": {"tm": tm, "tok": yh * 2 * ZG + lax.rem(z + 1, ZG) * 2 + c},
        "z-": {"tm": tm, "tok": yh * 2 * ZG + lax.rem(z + ZG - 1, ZG) * 2 + c},
        "core": {"tm": tm, "tok": yh * 2 * ZG + z * 2 + 1 - c},
        "part": {"tm": (1 - yl) * XG + x, "tok": (1 - yh) * 2 * ZG + z * 2 + c},
    }
    lower = {"tm": (1 - yl) * XG + x, "tok": tok}
    beside = at_tok(2 * c - 1)

    barrier = pltpu.get_barrier_semaphore()
    everyone = [at_x(1), at_x(2), at_x(3), *peers.values(), lower, beside]
    for peer in everyone:
        pl.semaphore_signal(barrier, inc=1, device_id=peer, device_id_type=MESH)
    pl.semaphore_wait(barrier, len(everyone))

    sent = []

    def remote(src, dst, s, r, i, peer):
        return pltpu.make_async_remote_copy(
            src_ref=src, dst_ref=dst, send_sem=s.at[i], recv_sem=r.at[i],
            device_id=peer, device_id_type=MESH,
        )

    def push(*args):
        copy = remote(*args)
        copy.start()
        sent.append(copy)

    top, bottom = pl.ds(0, part_rows), pl.ds(part_rows, part_rows)

    own_copies = []
    for j in range(3):
        column = pl.multiple_of(j * width + x * CW, HD)
        own_copies.append(pltpu.make_async_copy(
            wqkv_ref.at[:, pl.ds(column, CW)],
            wbuf.at[yh, z, c, :, pl.ds(j * CW, CW)], lsem.at[j],
        ))
    own_copies.append(pltpu.make_async_copy(wout_ref, wo.at[yh, z, c], lsem.at[3]))
    for copy in own_copies:
        copy.start()

    push(h_ref.at[top], hbuf.at[0, top], hs, hr, 0, at_x(1))
    push(h_ref.at[bottom], hbuf.at[0, bottom], hs, hr, 1, at_x(3))
    for copy in own_copies:
        copy.wait()
    pos = (yh, z, c)
    wring = Ring(wbuf, ws, wr, pos, peers)
    oring = Ring(wo, os, orecv, pos, peers)
    wring.own()
    push(h_ref.at[bottom], hbuf.at[1, top], hs, hr, 2, at_x(1))
    push(h_ref.at[top], hbuf.at[1, bottom], hs, hr, 3, at_x(3))

    def h_arrive(group):
        i = 2 * group
        remote(hbuf.at[group, top], hbuf.at[group, top], hs, hr, i, at_x(1)).wait_recv()
        remote(hbuf.at[group, bottom], hbuf.at[group, bottom], hs, hr, i + 1, at_x(3)).wait_recv()

    wring.step(1)
    wring.step(2)
    wring.step(3)
    h_arrive(0)
    push(hbuf.at[0, top], hbuf.at[2, top], hs, hr, 4, at_x(1))
    push(hbuf.at[0, bottom], hbuf.at[2, bottom], hs, hr, 5, at_x(3))
    wring.step(4)
    wring.share_own()
    oring.own()
    oring.step(1)
    oring.step(2)
    wring.share_other()
    wring.shared()

    kvs = (kv0, kv1, kv2, kv3)

    def qkv(group):
        kv = kvs[group]

        def one(j, carry):
            column = pl.multiple_of(j * CW, HD)
            left = h_ref[...] if group == 0 else hbuf[group - 1]
            right = wbuf[:, :, :, :, pl.ds(column, CW)].reshape(width, CW)
            part = jnp.dot(left, right, preferred_element_type=jnp.float32)
            pieces = []
            for head in range(HL):
                piece = part[:, head * HD : (head + 1) * HD]
                norm = lax.rsqrt(jnp.mean(piece * piece, -1, keepdims=True) + 1e-06)
                pieces.append(piece * jnp.where(j < 2, norm, 1.0))
            done = jnp.concatenate(pieces, axis=1).astype(jnp.bfloat16)
            for half in range(2):
                for tile in range(2):
                    first = half * part_rows + tile * TILE
                    kv[2 + tile, j, half] = done[first : first + TILE]
            return carry

        lax.fori_loop(0, 3, one, 0)
        push(kv.at[2:4, 1:3], kv.at[0:2, 1:3], ks, kr, 2 * group, at_tok(1))
        push(kv.at[2:4, 1:3], kv.at[4:6, 1:3], ks, kr, 2 * group + 1, at_tok(-1))

    def attend(group):
        kv = kvs[group]
        remote(kv.at[0:2, 1:3], kv.at[0:2, 1:3], ks, kr, 2 * group, at_tok(1)).wait_recv()
        remote(kv.at[4:6, 1:3], kv.at[4:6, 1:3], ks, kr, 2 * group + 1, at_tok(-1)).wait_recv()

        def one(i, carry):
            half, tile = lax.div(i, 2), lax.rem(i, 2)
            if group == 0:
                when = 2 * x + half
            elif group == 3:
                when = 2 * lax.rem(x + 2, XG) + half
            elif group == 1:
                when = 2 * lax.rem(x + 3 + 2 * half, XG) + half
            else:
                when = 2 * lax.rem(x + 3 + 2 * half, XG) + 1 - half
            step = step_ref[0, when]
            near = [
                jnp.clip(nb_ref[tile, n] - (2 * tok - 2), 0, 5) for n in range(nb_ref.shape[1])
            ]
            query = kv[2 + tile, 0, half]
            keys = jnp.concatenate([kv[n, 1, half] for n in near], axis=0)
            values = jnp.concatenate([kv[n, 2, half] for n in near], axis=0)
            outs = []
            for head in range(HL):
                cols = slice(head * HD, (head + 1) * HD)
                score = lax.dot_general(
                    query[:, cols], keys[:, cols], (((1,), (1,)), ((), ())),
                    preferred_element_type=jnp.float32,
                ) * (1.0 / math.sqrt(HD))
                expo = jnp.exp(score)
                total = jnp.sum(expo, -1, keepdims=True)
                mixed = jnp.dot(
                    expo.astype(jnp.bfloat16), values[:, cols], preferred_element_type=jnp.float32
                )
                outs.append(mixed * (step / total))
            abuf[when, pl.ds(pl.multiple_of(tile * TILE, TILE), TILE), :] = jnp.concatenate(
                outs, axis=1
            )
            return carry

        lax.fori_loop(0, 4, one, 0)

    qkv(0)
    oring.step(3)
    qkv(1)
    oring.step(4)
    oring.share_own()
    attend(0)
    h_arrive(1)
    qkv(2)
    attend(1)
    h_arrive(2)
    qkv(3)
    attend(2)
    attend(3)

    total = abuf[0]
    for k in range(1, 2 * XG):
        total = total + abuf[k]
    tsend[...] = total.astype(jnp.bfloat16)
    push(tsend, trecv, ts, tr, 0, lower)
    remote(trecv, trecv, ts, tr, 0, lower).wait_recv()
    run = jnp.where(yl > 0, trecv[...].astype(jnp.float32), 0.0)
    for k in range(2 * XG):
        sbuf[k] = run.astype(jnp.bfloat16)
        if k < 2 * XG - 1:
            run = run + abuf[k]

    def columns_of(src):
        return sall.at[:, :, pl.ds(pl.multiple_of(src * CW, HD), CW)]

    for k in range(1, XG):
        push(sbuf.at[pl.ds(2 * lax.rem(x + k, XG), 2)], columns_of(x), ss, sr, k - 1, at_x(k))
    keep = pltpu.make_async_copy(sbuf.at[pl.ds(2 * x, 2)], columns_of(x), lsem.at[4])
    keep.start()
    oring.share_other()
    oring.shared()
    keep.wait()
    for k in range(1, XG):
        source = columns_of(lax.rem(x + XG - k, XG))
        remote(source, source, ss, sr, k - 1, at_x(k)).wait_recv()

    chunk = 256

    def finish(i, carry):
        column = pl.ds(pl.multiple_of(i * chunk, chunk), chunk)
        left = sall[...].reshape(rows, width)
        right = wo[:, :, :, :, column].reshape(width, chunk)
        before = jnp.dot(left, right, preferred_element_type=jnp.float32)
        first = start_ref[:, column].astype(jnp.float32)
        out_ref[0, :, column] = first - before[:part_rows]
        out_ref[1, :, column] = first - before[part_rows:]
        return carry

    lax.fori_loop(0, width // chunk, finish, 0)
    wring.finish()
    oring.finish()
    for copy in sent:
        copy.wait_send()


def body(start, trajectory, plan, neighbors, mod_weight, w_qkv, w_out):
    steps_here, tok_here, width = trajectory.shape
    rows = steps_here * tok_here
    times = plan.astype(jnp.float32) / NSCHED
    steps = times[:-1] - times[1:]
    tm = lax.axis_index("tm")
    own_times = lax.dynamic_slice_in_dim(times, tm * steps_here, steps_here)
    ring_steps = lax.dynamic_slice_in_dim(
        steps, lax.div(tm, XG) * XG * steps_here, XG * steps_here
    )[None]
    mod = time_mod(own_times, mod_weight)
    h = modulate(trajectory, mod[:, None, :width], mod[:, None, width:]).reshape(rows, width)
    bf, f32 = jnp.bfloat16, jnp.float32
    kv = pltpu.VMEM((6, 3, steps_here, TILE, CW), bf)
    dma = pltpu.SemaphoreType.DMA
    vmem = pl.BlockSpec(memory_space=pltpu.VMEM)
    smem = pl.BlockSpec(memory_space=pltpu.SMEM)
    hbm = pl.BlockSpec(memory_space=pl.ANY)
    return pl.pallas_call(
        kernel,
        out_shape=jax.ShapeDtypeStruct((steps_here, tok_here, width), f32),
        in_specs=[vmem, hbm, hbm, vmem, smem, smem],
        out_specs=vmem,
        scratch_shapes=[
            pltpu.VMEM((3, rows, width), bf),
            pltpu.VMEM((2, ZG, 2, w_qkv.shape[0], 3 * CW), bf),
            pltpu.VMEM((2, ZG, 2, w_out.shape[0], width), bf),
            kv, kv, kv, kv,
            pltpu.VMEM((2 * XG, tok_here, CW), f32),
            pltpu.VMEM((tok_here, CW), bf),
            pltpu.VMEM((tok_here, CW), bf),
            pltpu.VMEM((2 * XG, tok_here, CW), bf),
            pltpu.VMEM((steps_here, tok_here, width), bf),
            dma((5,)),
            dma((6,)), dma((6,)),
            dma((17,)), dma((17,)),
            dma((17,)), dma((17,)),
            dma((8,)), dma((8,)),
            dma((1,)), dma((1,)),
            dma((3,)), dma((3,)),
        ],
        compiler_params=pltpu.CompilerParams(collective_id=0, has_side_effects=True),
    )(h, w_qkv, w_out, start, neighbors, ring_steps)


def solution(mesh):
    return jax.shard_map(
        body,
        mesh=mesh,
        in_specs=(
            P("tok", None),
            P("tm", "tok", None),
            P(),
            P("tok", None),
            P(),
            P("tok", None),
            P("tok", None),
        ),
        out_specs=P("tm", "tok", None),
        check_vma=False,
    )
```

```python
import functools
import math

import jax
import jax.numpy as jnp
from jax import lax
from jax.experimental import pallas as pl
from jax.experimental.pallas import tpu as pltpu
from jax.sharding import PartitionSpec as P

NSCHED = 1000
XG = 4
ZG = 8
HL = 3
HD = 128
CW = HL * HD
TILE = 64
MESH = pl.DeviceIdType.MESH


def time_mod(times, mod_weight):
    half = mod_weight.shape[0] // 2
    freqs = jnp.exp(-math.log(10000.0) * jnp.arange(half, dtype=jnp.float32) / half)
    angle = 1000.0 * times[:, None] * freqs[None, :]
    embed = jnp.concatenate([jnp.cos(angle), jnp.sin(angle)], axis=1)
    act = jax.nn.silu(embed).astype(jnp.bfloat16)
    return jnp.dot(act, mod_weight, preferred_element_type=jnp.float32)


def modulate(state, shift, scale):
    values = state.astype(jnp.float32)
    center = values - jnp.mean(values, -1, keepdims=True)
    spread = jnp.mean(center * center, -1, keepdims=True)
    return (center / jnp.sqrt(spread + 1e-06) * (1.0 + scale) + shift).astype(jnp.bfloat16)


class Ring:
    eager = True

    def __init__(self, buf, cols, send, recv, base, pos, peers):
        self.buf, self.cols = buf, cols
        self.send, self.recv, self.base = send, recv, base
        self.yl, self.yh, self.z, self.c = pos
        self.peers = peers
        self.sent = []

    def block(self, yh, off, full=False, other=False):
        ref = self.buf.at[yh, lax.rem(self.z + off, ZG), 1 - self.c if other else self.c]
        return ref if full else ref.at[:, self.cols]

    def slot(self, k, yl):
        return yl * (0, 2, 6, 4)[k] + (1 - yl) * (1, 7, 3, 5)[k]

    def copy(self, ref, i, peer):
        i = self.base + i
        return pltpu.make_async_remote_copy(
            src_ref=ref, dst_ref=ref, send_sem=self.send.at[i], recv_sem=self.recv.at[i],
            device_id=self.peers[peer], device_id_type=MESH,
        )

    def push(self, ref, i, peer):
        copy = self.copy(ref, i, peer)
        copy.start()
        self.sent.append(copy)

    def arrive(self, ref, i, peer):
        self.copy(ref, i, peer).wait_recv()

    def give(self, yh, off, i):
        self.push(self.block(yh, off), i, "core")

    def own(self):
        mine = self.block(self.yh, 0)
        self.push(mine, 0, "z+")
        self.push(mine, 4, "z-")
        self.give(self.yh, 0, 15)

    def step(self, s):
        low = self.block(self.yh, ZG - s)
        self.arrive(low, s - 1, "z+")
        if s < 4:
            self.push(low, s, "z+")
            high = self.block(self.yh, s)
            self.arrive(high, 3 + s, "z-")
            if s < 3:
                self.push(high, 4 + s, "z-")
        if self.eager:
            self.push(self.block(self.yh, self.slot(s - 1, self.yl)), 6 + s, "part")
        self.give(self.yh, ZG - s, 15 + ZG - s)
        if s < 4:
            self.give(self.yh, s, 15 + s)

    def relay(self, k):
        off = self.slot(k, 1 - self.yl)
        self.arrive(self.block(1 - self.yh, off), 7 + k, "part")
        self.push(self.block(1 - self.yh, off), 11 + k, "low")
        self.give(1 - self.yh, off, 23 + k)

    def collect(self, k):
        off = self.slot(k, self.yl)
        self.arrive(self.block(1 - self.yh, off), 11 + k, "low")
        self.give(1 - self.yh, off, 27 + k)

    def shared(self):
        for off in range(ZG):
            self.arrive(self.block(self.yh, off, other=True), 15 + off, "core")
        for k in range(4):
            for i, yl in ((23, 1 - self.yl), (27, self.yl)):
                off = self.slot(k, yl)
                self.arrive(self.block(1 - self.yh, off, other=True), i + k, "core")

    def finish(self):
        for copy in self.sent:
            copy.wait_send()


class WideRing(Ring):
    eager = False

    def part(self, k):
        self.push(self.block(self.yh, self.slot(k, self.yl)), 7 + k, "part")

    def give(self, yh, off, i):
        pass

    def whole(self, yh, c, other=False):
        return self.buf.at[yh, :, c, :, self.rest if other else self.cols]

    def swap(self):
        self.push(self.whole(self.yh, self.c), 15, "x+")
        self.push(self.whole(1 - self.yh, self.c), 16, "x-")
        self.push(self.whole(self.yh, self.c), 17, "core")
        self.push(self.whole(1 - self.yh, self.c), 18, "core")

    def swapped(self):
        self.arrive(self.whole(self.yh, self.c, True), 15, "x+")
        self.push(self.whole(self.yh, self.c, True), 19, "core")
        self.arrive(self.whole(1 - self.yh, self.c, True), 16, "x-")
        self.push(self.whole(1 - self.yh, self.c, True), 20, "core")

    def shared(self):
        c = 1 - self.c
        self.arrive(self.whole(self.yh, c), 17, "core")
        self.arrive(self.whole(1 - self.yh, c), 18, "core")
        self.arrive(self.whole(self.yh, c, True), 19, "core")
        self.arrive(self.whole(1 - self.yh, c, True), 20, "core")


def kernel(
    h_ref, wqkv_ref, wout_ref, start_ref, nb_ref, step_ref, out_ref,
    hbuf, wbuf, wo, kv0, kv1, kv2, kv3, abuf, tsend, trecv, sbuf, sall,
    lsem, hs, hr, ws, wr, os, orecv, ks, kr, ts, tr, ss, sr,
):
    tm, tok = lax.axis_index("tm"), lax.axis_index("tok")
    x, yl = lax.rem(tm, XG), lax.div(tm, XG)
    yh, z, c = lax.div(tok, 2 * ZG), lax.div(lax.rem(tok, 2 * ZG), 2), lax.rem(tok, 2)
    width = h_ref.shape[1]
    rows = h_ref.shape[0]
    part_rows = rows // 2
    ntok = 4 * ZG

    def at_x(k):
        return {"tm": yl * XG + lax.rem(x + k, XG), "tok": tok}

    def at_tok(k):
        return {"tm": tm, "tok": lax.rem(tok + ntok + k, ntok)}

    peers = {
        "z+": {"tm": tm, "tok": yh * 2 * ZG + lax.rem(z + 1, ZG) * 2 + c},
        "z-": {"tm": tm, "tok": yh * 2 * ZG + lax.rem(z + ZG - 1, ZG) * 2 + c},
        "core": {"tm": tm, "tok": yh * 2 * ZG + z * 2 + 1 - c},
        "part": {"tm": (1 - yl) * XG + x, "tok": (1 - yh) * 2 * ZG + z * 2 + c},
        "low": {"tm": (1 - yl) * XG + x, "tok": tok},
        "x+": at_x(1),
        "x-": at_x(3),
    }
    lower = peers["low"]
    beside = at_tok(2 * c - 1)

    own_copies = []
    for j in range(3):
        column = pl.multiple_of(j * width + x * CW, HD)
        own_copies.append(pltpu.make_async_copy(
            wqkv_ref.at[:, pl.ds(column, CW)],
            wbuf.at[yh, z, c, :, pl.ds((j + 2) % 3 * CW, CW)], lsem.at[j],
        ))
    own_copies.append(pltpu.make_async_copy(wout_ref, wo.at[yh, z, c], lsem.at[3]))
    for copy in own_copies:
        copy.start()

    barrier = pltpu.get_barrier_semaphore()
    everyone = [at_x(2), *peers.values(), beside]
    for peer in everyone:
        pl.semaphore_signal(barrier, inc=1, device_id=peer, device_id_type=MESH)
    pl.semaphore_wait(barrier, len(everyone))

    sent = []

    def remote(src, dst, s, r, i, peer):
        return pltpu.make_async_remote_copy(
            src_ref=src, dst_ref=dst, send_sem=s.at[i], recv_sem=r.at[i],
            device_id=peer, device_id_type=MESH,
        )

    def push(*args):
        copy = remote(*args)
        copy.start()
        sent.append(copy)

    top, bottom = pl.ds(0, part_rows), pl.ds(part_rows, part_rows)

    push(h_ref.at[top], hbuf.at[0, top], hs, hr, 0, at_x(1))
    push(h_ref.at[bottom], hbuf.at[0, bottom], hs, hr, 1, at_x(3))
    for copy in own_copies:
        copy.wait()
    pos = (yl, yh, z, c)
    cut = 2 * CW
    wfirst = Ring(wbuf, pl.ds(0, cut), ws, wr, 0, pos, peers)
    wlast = Ring(wbuf, pl.ds(cut, 3 * CW - cut), ws, wr, 31, pos, peers)
    parity = lax.rem(x, 2)
    span = width // 2

    def wide(i):
        return pl.ds(pl.multiple_of(i * span, HD), span)

    oring = WideRing(wo, wide(parity), os, orecv, 0, pos, peers)
    oring.rest = wide(1 - parity)
    wfirst.own()
    wlast.own()
    oring.own()
    push(h_ref.at[bottom], hbuf.at[1, top], hs, hr, 2, at_x(1))
    push(h_ref.at[top], hbuf.at[1, bottom], hs, hr, 3, at_x(3))

    def h_arrive(group):
        i = 2 * group
        remote(hbuf.at[group, top], hbuf.at[group, top], hs, hr, i, at_x(1)).wait_recv()
        remote(hbuf.at[group, bottom], hbuf.at[group, bottom], hs, hr, i + 1, at_x(3)).wait_recv()

    wfirst.step(1)
    wlast.step(1)
    oring.step(1)
    oring.part(0)
    wfirst.step(2)
    wlast.step(2)
    wfirst.relay(0)
    wlast.relay(0)
    oring.step(2)
    oring.part(1)
    wfirst.step(3)
    wlast.step(3)
    h_arrive(0)
    push(hbuf.at[0, top], hbuf.at[2, top], hs, hr, 4, at_x(1))
    push(hbuf.at[0, bottom], hbuf.at[2, bottom], hs, hr, 5, at_x(3))
    wfirst.relay(1)
    wlast.relay(1)
    wfirst.collect(0)
    wlast.collect(0)
    oring.step(3)
    oring.part(2)
    oring.relay(0)
    wfirst.step(4)
    wlast.step(4)
    wfirst.relay(2)
    wlast.relay(2)
    wfirst.collect(1)
    wlast.collect(1)
    oring.step(4)
    oring.part(3)
    oring.relay(1)
    wfirst.relay(3)
    wlast.relay(3)
    oring.relay(2)
    wfirst.collect(2)
    wlast.collect(2)
    oring.collect(0)
    wfirst.collect(3)
    wlast.collect(3)
    oring.relay(3)
    wfirst.shared()

    kvs = (kv0, kv1, kv2, kv3)

    def project(group, first, last):
        kv = kvs[group]

        def one(j, carry):
            column = pl.multiple_of(j * CW, HD)
            left = h_ref[...] if group == 0 else hbuf[group - 1]
            right = wbuf[:, :, :, :, pl.ds(column, CW)].reshape(width, CW)
            part = jnp.dot(left, right, preferred_element_type=jnp.float32)
            pieces = []
            for head in range(HL):
                piece = part[:, head * HD : (head + 1) * HD]
                norm = lax.rsqrt(jnp.mean(piece * piece, -1, keepdims=True) + 1e-06)
                pieces.append(piece * jnp.where(j == 1, 1.0, norm))
            done = jnp.concatenate(pieces, axis=1).astype(jnp.bfloat16)
            for half in range(2):
                for tile in range(2):
                    row = half * part_rows + tile * TILE
                    kv[2 + tile, j, half] = done[row : row + TILE]
            return carry

        lax.fori_loop(first, last, one, 0)

    def halo(group):
        kv = kvs[group]
        mine = kv.at[2:4, 0:2]
        return (
            remote(mine, kv.at[0:2, 0:2], ks, kr, 2 * group, at_tok(1)),
            remote(mine, kv.at[4:6, 0:2], ks, kr, 2 * group + 1, at_tok(-1)),
        )

    def keys_values(group):
        project(group, 0, 2)
        ahead, behind = halo(group)

        @pl.when(tok < ntok - 1)
        def _():
            ahead.start()

        @pl.when(tok > 0)
        def _():
            behind.start()

    def attend(group):
        kv = kvs[group]
        ahead, behind = halo(group)

        @pl.when(tok > 0)
        def _():
            ahead.wait_recv()

        @pl.when(tok < ntok - 1)
        def _():
            behind.wait_recv()


        def one(i, carry):
            half, tile = lax.div(i, 2), lax.rem(i, 2)
            if group == 0:
                when = 2 * x + half
            elif group == 3:
                when = 2 * lax.rem(x + 2, XG) + half
            elif group == 1:
                when = 2 * lax.rem(x + 3 + 2 * half, XG) + half
            else:
                when = 2 * lax.rem(x + 3 + 2 * half, XG) + 1 - half
            step = step_ref[0, when]
            near = [
                jnp.clip(nb_ref[tile, n] - (2 * tok - 2), 0, 5) for n in range(nb_ref.shape[1])
            ]
            query = kv[2 + tile, 2, half]
            keys = jnp.concatenate([kv[n, 0, half] for n in near], axis=0)
            values = jnp.concatenate([kv[n, 1, half] for n in near], axis=0)
            outs = []
            for head in range(HL):
                cols = slice(head * HD, (head + 1) * HD)
                score = lax.dot_general(
                    query[:, cols], keys[:, cols], (((1,), (1,)), ((), ())),
                    preferred_element_type=jnp.float32,
                ) * (1.0 / math.sqrt(HD))
                expo = jnp.exp(score)
                total = jnp.sum(expo, -1, keepdims=True)
                mixed = jnp.dot(
                    expo.astype(jnp.bfloat16), values[:, cols], preferred_element_type=jnp.float32
                )
                outs.append(mixed * (step / total))
            abuf[when, pl.ds(pl.multiple_of(tile * TILE, TILE), TILE), :] = jnp.concatenate(
                outs, axis=1
            )
            return carry

        lax.fori_loop(0, 4, one, 0, unroll=2)

    keys_values(0)
    keys_values(1)
    h_arrive(1)
    keys_values(2)
    h_arrive(2)
    keys_values(3)
    wlast.shared()
    project(0, 2, 3)
    project(1, 2, 3)
    project(2, 2, 3)
    project(3, 2, 3)
    oring.collect(1)
    oring.collect(2)
    oring.collect(3)
    oring.swap()
    attend(0)
    attend(1)
    attend(2)
    attend(3)

    total = abuf[0]
    for k in range(1, 2 * XG):
        total = total + abuf[k]
    tsend[...] = total.astype(jnp.bfloat16)
    push(tsend, trecv, ts, tr, 0, lower)
    remote(trecv, trecv, ts, tr, 0, lower).wait_recv()
    run = jnp.where(yl > 0, trecv[...].astype(jnp.float32), 0.0)
    for k in range(2 * XG):
        sbuf[k] = run.astype(jnp.bfloat16)
        if k < 2 * XG - 1:
            run = run + abuf[k]

    def columns_of(src):
        return sall.at[:, :, pl.ds(pl.multiple_of(src * CW, HD), CW)]

    for k in range(1, XG):
        push(sbuf.at[pl.ds(2 * lax.rem(x + k, XG), 2)], columns_of(x), ss, sr, k - 1, at_x(k))
    keep = pltpu.make_async_copy(sbuf.at[pl.ds(2 * x, 2)], columns_of(x), lsem.at[4])
    keep.start()
    oring.swapped()
    oring.shared()
    keep.wait()
    for k in range(1, XG):
        source = columns_of(lax.rem(x + XG - k, XG))
        remote(source, source, ss, sr, k - 1, at_x(k)).wait_recv()

    chunk = 256

    def finish(i, carry):
        column = pl.ds(pl.multiple_of(i * chunk, chunk), chunk)
        left = sall[...].reshape(rows, width)
        right = wo[:, :, :, :, column].reshape(width, chunk)
        before = jnp.dot(left, right, preferred_element_type=jnp.float32)
        first = start_ref[:, column].astype(jnp.float32)
        out_ref[0, :, column] = first - before[:part_rows]
        out_ref[1, :, column] = first - before[part_rows:]
        return carry

    lax.fori_loop(0, width // chunk, finish, 0)
    wfirst.finish()
    wlast.finish()
    oring.finish()
    for group in range(4):
        ahead, behind = halo(group)

        @pl.when(tok < ntok - 1)
        def _():
            ahead.wait_send()

        @pl.when(tok > 0)
        def _():
            behind.wait_send()

    for copy in sent:
        copy.wait_send()


def body(start, trajectory, plan, neighbors, mod_weight, w_qkv, w_out):
    steps_here, tok_here, width = trajectory.shape
    rows = steps_here * tok_here
    times = plan.astype(jnp.float32) / NSCHED
    steps = times[:-1] - times[1:]
    tm = lax.axis_index("tm")
    own_times = lax.dynamic_slice_in_dim(times, tm * steps_here, steps_here)
    ring_steps = lax.dynamic_slice_in_dim(
        steps, lax.div(tm, XG) * XG * steps_here, XG * steps_here
    )[None]
    mod = time_mod(own_times, mod_weight)
    h = modulate(trajectory, mod[:, None, :width], mod[:, None, width:]).reshape(rows, width)
    bf, f32 = jnp.bfloat16, jnp.float32
    kv = pltpu.VMEM((6, 3, steps_here, TILE, CW), bf)
    dma = pltpu.SemaphoreType.DMA
    vmem = pl.BlockSpec(memory_space=pltpu.VMEM)
    smem = pl.BlockSpec(memory_space=pltpu.SMEM)
    hbm = pl.BlockSpec(memory_space=pl.ANY)
    return pl.pallas_call(
        kernel,
        out_shape=jax.ShapeDtypeStruct((steps_here, tok_here, width), f32),
        in_specs=[vmem, hbm, hbm, vmem, smem, smem],
        out_specs=vmem,
        scratch_shapes=[
            pltpu.VMEM((3, rows, width), bf),
            pltpu.VMEM((2, ZG, 2, w_qkv.shape[0], 3 * CW), bf),
            pltpu.VMEM((2, ZG, 2, w_out.shape[0], width), bf),
            kv, kv, kv, kv,
            pltpu.VMEM((2 * XG, tok_here, CW), f32),
            pltpu.VMEM((tok_here, CW), bf),
            pltpu.VMEM((tok_here, CW), bf),
            pltpu.VMEM((2 * XG, tok_here, CW), bf),
            pltpu.VMEM((steps_here, tok_here, width), bf),
            dma((5,)),
            dma((6,)), dma((6,)),
            dma((62,)), dma((62,)),
            dma((21,)), dma((21,)),
            dma((8,)), dma((8,)),
            dma((1,)), dma((1,)),
            dma((3,)), dma((3,)),
        ],
        compiler_params=pltpu.CompilerParams(collective_id=0, has_side_effects=True),
    )(h, w_qkv, w_out, start, neighbors, ring_steps)


def solution(mesh):
    return jax.shard_map(
        body,
        mesh=mesh,
        in_specs=(
            P("tok", None),
            P("tm", "tok", None),
            P(),
            P("tok", None),
            P(),
            P("tok", None),
            P("tok", None),
        ),
        out_specs=P("tm", "tok", None),
        check_vma=False,
    )
```

```python
import math

import jax
import jax.numpy as jnp
from jax import lax
from jax.experimental import pallas as pl
from jax.experimental.pallas import tpu as pltpu
from jax.sharding import PartitionSpec as P

NSCHED = 1000
XG = 4
ZG = 8
HL = 3
HD = 128
CW = HL * HD
TILE = 64
MESH = pl.DeviceIdType.MESH


class Ring:
    eager = True

    def __init__(self, buf, cols, send, recv, base, pos, peers):
        self.buf, self.cols = buf, cols
        self.send, self.recv, self.base = send, recv, base
        self.yl, self.yh, self.z, self.c = pos
        self.peers = peers
        self.sent = []

    def block(self, yh, off, full=False, other=False):
        ref = self.buf.at[yh, lax.rem(self.z + off, ZG), 1 - self.c if other else self.c]
        return ref if full else ref.at[:, self.cols]

    def slot(self, k, yl):
        return yl * (0, 2, 6, 4)[k] + (1 - yl) * (1, 7, 3, 5)[k]

    def copy(self, ref, i, peer):
        i = self.base + i
        return pltpu.make_async_remote_copy(
            src_ref=ref, dst_ref=ref, send_sem=self.send.at[i], recv_sem=self.recv.at[i],
            device_id=self.peers[peer], device_id_type=MESH,
        )

    def push(self, ref, i, peer):
        copy = self.copy(ref, i, peer)
        copy.start()
        self.sent.append(copy)

    def arrive(self, ref, i, peer):
        self.copy(ref, i, peer).wait_recv()

    def give(self, yh, off, i):
        self.push(self.block(yh, off), i, "core")

    def own(self):
        mine = self.block(self.yh, 0)
        self.push(mine, 0, "z+")
        self.push(mine, 4, "z-")
        self.give(self.yh, 0, 15)

    def step(self, s):
        low = self.block(self.yh, ZG - s)
        self.arrive(low, s - 1, "z+")
        if s < 4:
            self.push(low, s, "z+")
            high = self.block(self.yh, s)
            self.arrive(high, 3 + s, "z-")
            if s < 3:
                self.push(high, 4 + s, "z-")
        if self.eager:
            self.push(self.block(self.yh, self.slot(s - 1, self.yl)), 6 + s, "part")
        self.give(self.yh, ZG - s, 15 + ZG - s)
        if s < 4:
            self.give(self.yh, s, 15 + s)

    def relay(self, k):
        off = self.slot(k, 1 - self.yl)
        self.arrive(self.block(1 - self.yh, off), 7 + k, "part")
        self.push(self.block(1 - self.yh, off), 11 + k, "low")
        self.give(1 - self.yh, off, 23 + k)

    def collect(self, k):
        off = self.slot(k, self.yl)
        self.arrive(self.block(1 - self.yh, off), 11 + k, "low")
        self.give(1 - self.yh, off, 27 + k)

    def shared(self):
        for off in range(ZG):
            self.arrive(self.block(self.yh, off, other=True), 15 + off, "core")
        for k in range(4):
            for i, yl in ((23, 1 - self.yl), (27, self.yl)):
                off = self.slot(k, yl)
                self.arrive(self.block(1 - self.yh, off, other=True), i + k, "core")

    def finish(self):
        for copy in self.sent:
            copy.wait_send()


class WideRing(Ring):
    eager = False

    def part(self, k):
        self.push(self.block(self.yh, self.slot(k, self.yl)), 7 + k, "part")

    def give(self, yh, off, i):
        pass

    def whole(self, yh, c, other=False):
        return self.buf.at[yh, :, c, :, self.rest if other else self.cols]

    def swap(self):
        self.push(self.whole(self.yh, self.c), 15, "x+")
        self.push(self.whole(1 - self.yh, self.c), 16, "x-")
        self.push(self.whole(self.yh, self.c), 17, "core")
        self.push(self.whole(1 - self.yh, self.c), 18, "core")

    def swapped(self):
        self.arrive(self.whole(self.yh, self.c, True), 15, "x+")
        self.push(self.whole(self.yh, self.c, True), 19, "core")
        self.arrive(self.whole(1 - self.yh, self.c, True), 16, "x-")
        self.push(self.whole(1 - self.yh, self.c, True), 20, "core")

    def shared(self):
        c = 1 - self.c
        self.arrive(self.whole(self.yh, c), 17, "core")
        self.arrive(self.whole(1 - self.yh, c), 18, "core")
        self.arrive(self.whole(self.yh, c, True), 19, "core")
        self.arrive(self.whole(1 - self.yh, c, True), 20, "core")


def kernel(
    x_ref, plan_ref, freq_ref, mod_ref, wqkv_ref, wout_ref, start_hbm, nb_ref, out_ref,
    start_ref, own, modw, mods, hbuf, hnorm, wbuf, wo, kv0, kv1, kv2, kv3, abuf, tsend, trecv, sbuf, sall,
    lsem, hs, hr, ws, wr, os, orecv, ks, kr, ts, tr, ss, sr,
):
    tm, tok = lax.axis_index("tm"), lax.axis_index("tok")
    x, yl = lax.rem(tm, XG), lax.div(tm, XG)
    yh, z, c = lax.div(tok, 2 * ZG), lax.div(lax.rem(tok, 2 * ZG), 2), lax.rem(tok, 2)
    part_rows, width = x_ref.shape[1:]
    rows = 2 * part_rows
    ntok = 4 * ZG

    def at_x(k):
        return {"tm": yl * XG + lax.rem(x + k, XG), "tok": tok}

    def at_tok(k):
        return {"tm": tm, "tok": lax.rem(tok + ntok + k, ntok)}

    peers = {
        "z+": {"tm": tm, "tok": yh * 2 * ZG + lax.rem(z + 1, ZG) * 2 + c},
        "z-": {"tm": tm, "tok": yh * 2 * ZG + lax.rem(z + ZG - 1, ZG) * 2 + c},
        "core": {"tm": tm, "tok": yh * 2 * ZG + z * 2 + 1 - c},
        "part": {"tm": (1 - yl) * XG + x, "tok": (1 - yh) * 2 * ZG + z * 2 + c},
        "low": {"tm": (1 - yl) * XG + x, "tok": tok},
        "x+": at_x(1),
        "x-": at_x(3),
    }
    lower = peers["low"]
    beside = at_tok(2 * c - 1)

    own_copies = []
    for j in range(3):
        column = pl.multiple_of(j * width + x * CW, HD)
        own_copies.append(pltpu.make_async_copy(
            wqkv_ref.at[:, pl.ds(column, CW)],
            wbuf.at[yh, z, c, :, pl.ds((j + 2) % 3 * CW, CW)], lsem.at[j],
        ))
    own_copies.append(pltpu.make_async_copy(wout_ref, wo.at[yh, z, c], lsem.at[3]))
    state_copies = [
        pltpu.make_async_copy(x_ref, own, lsem.at[5]),
        pltpu.make_async_copy(mod_ref, modw, lsem.at[6]),
        pltpu.make_async_copy(start_hbm, start_ref, lsem.at[7]),
    ]
    for copy in own_copies + state_copies:
        copy.start()

    barrier = pltpu.get_barrier_semaphore()
    everyone = [at_x(2), *peers.values(), beside]
    for peer in everyone:
        pl.semaphore_signal(barrier, inc=1, device_id=peer, device_id_type=MESH)
    pl.semaphore_wait(barrier, len(everyone))

    sent = []

    def remote(src, dst, s, r, i, peer):
        return pltpu.make_async_remote_copy(
            src_ref=src, dst_ref=dst, send_sem=s.at[i], recv_sem=r.at[i],
            device_id=peer, device_id_type=MESH,
        )

    def push(*args):
        copy = remote(*args)
        copy.start()
        sent.append(copy)

    top, bottom = pl.ds(0, part_rows), pl.ds(part_rows, part_rows)

    push(x_ref.at[0], hbuf.at[0, top], hs, hr, 0, at_x(1))
    push(x_ref.at[1], hbuf.at[0, bottom], hs, hr, 1, at_x(3))
    for copy in own_copies:
        copy.wait()
    pos = (yl, yh, z, c)
    cut = 2 * CW
    wfirst = Ring(wbuf, pl.ds(0, cut), ws, wr, 0, pos, peers)
    wlast = Ring(wbuf, pl.ds(cut, 3 * CW - cut), ws, wr, 31, pos, peers)
    parity = lax.rem(x, 2)
    span = width // 2

    def wide(i):
        return pl.ds(pl.multiple_of(i * span, HD), span)

    oring = WideRing(wo, wide(parity), os, orecv, 0, pos, peers)
    oring.rest = wide(1 - parity)
    wfirst.own()
    wlast.own()
    oring.own()
    push(x_ref.at[1], hbuf.at[1, top], hs, hr, 2, at_x(1))
    push(x_ref.at[0], hbuf.at[1, bottom], hs, hr, 3, at_x(3))

    def h_arrive(group):
        i = 2 * group
        remote(hbuf.at[group, top], hbuf.at[group, top], hs, hr, i, at_x(1)).wait_recv()
        remote(hbuf.at[group, bottom], hbuf.at[group, bottom], hs, hr, i + 1, at_x(3)).wait_recv()

    def timestep(group, half):
        if group == 0:
            return 2 * x + half
        if group == 3:
            return 2 * lax.rem(x + 2, XG) + half
        owner = lax.rem(x + 3 + 2 * half, XG)
        return 2 * owner + (half if group == 1 else 1 - half)

    def plan_row(k, shape):
        return jnp.full(shape, plan_ref[yl * 2 * XG + k].astype(jnp.float32)) / NSCHED

    def time_of(k):
        return plan_row(k, (1, HD))

    def modulation():
        times = jnp.concatenate([plan_row(k, (1, freq_ref.shape[1])) for k in range(2 * XG)], axis=0)
        angle = 1000.0 * times * freq_ref[...]
        embed = jnp.concatenate([jnp.cos(angle), jnp.sin(angle)], axis=1)
        act = (embed / (1.0 + jnp.exp(-embed))).astype(jnp.bfloat16)
        mods[...] = jnp.dot(act, modw[...], preferred_element_type=jnp.float32)

    band = 16

    def norm(group):
        def one(i, carry):
            half, row = lax.div(i, part_rows // band), lax.rem(i, part_rows // band) * band
            at = pl.ds(pl.multiple_of(row, band), band)
            if group == 0:
                values = own[half, at, :]
            else:
                at_row = pl.multiple_of(i * band, band)
                values = hbuf[group - 1, pl.ds(at_row, band), :]
            values = values.astype(jnp.float32)
            when = timestep(group, half)
            shift = mods[pl.ds(when, 1), :width]
            scale = mods[pl.ds(when, 1), width:]
            center = values - jnp.mean(values, -1, keepdims=True)
            spread = jnp.mean(center * center, -1, keepdims=True)
            done = center * lax.rsqrt(spread + 1e-06) * (1.0 + scale) + shift
            hnorm[group, pl.ds(pl.multiple_of(i * band, band), band), :] = done.astype(jnp.bfloat16)
            return carry

        lax.fori_loop(0, rows // band, one, 0, unroll=4)

    for copy in state_copies:
        copy.wait()
    modulation()
    norm(0)
    wfirst.step(1)
    wlast.step(1)
    oring.step(1)
    oring.part(0)
    wfirst.step(2)
    wlast.step(2)
    wfirst.relay(0)
    wlast.relay(0)
    oring.step(2)
    oring.part(1)
    wfirst.step(3)
    wlast.step(3)
    h_arrive(0)
    push(hbuf.at[0, top], hbuf.at[2, top], hs, hr, 4, at_x(1))
    push(hbuf.at[0, bottom], hbuf.at[2, bottom], hs, hr, 5, at_x(3))
    norm(1)
    wfirst.relay(1)
    wlast.relay(1)
    wfirst.collect(0)
    wlast.collect(0)
    oring.step(3)
    oring.part(2)
    oring.relay(0)
    wfirst.step(4)
    wlast.step(4)
    wfirst.relay(2)
    wlast.relay(2)
    wfirst.collect(1)
    wlast.collect(1)
    oring.step(4)
    oring.part(3)
    oring.relay(1)
    wfirst.relay(3)
    wlast.relay(3)
    oring.relay(2)
    h_arrive(1)
    norm(2)
    wfirst.collect(2)
    wlast.collect(2)
    oring.collect(0)
    wfirst.collect(3)
    wlast.collect(3)
    oring.relay(3)
    wfirst.shared()

    kvs = (kv0, kv1, kv2, kv3)

    def project(group, first, last):
        kv = kvs[group]

        def one(j, carry):
            column = pl.multiple_of(j * CW, HD)
            left = hnorm[group]
            right = wbuf[:, :, :, :, pl.ds(column, CW)].reshape(width, CW)
            part = jnp.dot(left, right, preferred_element_type=jnp.float32)
            pieces = []
            for head in range(HL):
                piece = part[:, head * HD : (head + 1) * HD]
                norm = lax.rsqrt(jnp.mean(piece * piece, -1, keepdims=True) + 1e-06)
                pieces.append(piece * jnp.where(j == 1, 1.0, norm))
            done = jnp.concatenate(pieces, axis=1).astype(jnp.bfloat16)
            for half in range(2):
                for tile in range(2):
                    row = half * part_rows + tile * TILE
                    kv[2 + tile, j, half] = done[row : row + TILE]
            return carry

        lax.fori_loop(first, last, one, 0)

    def halo(group, j):
        mine = kvs[group].at[2:4, j]
        i = 4 * group + 2 * j
        return (
            remote(mine, kvs[group].at[0:2, j], ks, kr, i, at_tok(1)),
            remote(mine, kvs[group].at[4:6, j], ks, kr, i + 1, at_tok(-1)),
        )

    def keys_values(group):
        for j in range(2):
            project(group, j, j + 1)
            ahead, behind = halo(group, j)

            @pl.when(tok < ntok - 1)
            def _():
                ahead.start()

            @pl.when(tok > 0)
            def _():
                behind.start()

    def attend(group):
        kv = kvs[group]
        copies = [halo(group, j) for j in range(2)]

        @pl.when(tok > 0)
        def _():
            for ahead, _ in copies:
                ahead.wait_recv()

        @pl.when(tok < ntok - 1)
        def _():
            for _, behind in copies:
                behind.wait_recv()


        def one(i, carry):
            half, tile = lax.div(i, 2), lax.rem(i, 2)
            when = timestep(group, half)
            step = time_of(when) - time_of(when + 1)
            near = [
                jnp.clip(nb_ref[tile, n] - (2 * tok - 2), 0, 5) for n in range(nb_ref.shape[1])
            ]
            query = kv[2 + tile, 2, half]
            keys = jnp.concatenate([kv[n, 0, half] for n in near], axis=0)
            values = jnp.concatenate([kv[n, 1, half] for n in near], axis=0)
            outs = []
            for head in range(HL):
                cols = slice(head * HD, (head + 1) * HD)
                score = lax.dot_general(
                    query[:, cols], keys[:, cols], (((1,), (1,)), ((), ())),
                    preferred_element_type=jnp.float32,
                ) * (1.0 / math.sqrt(HD))
                expo = jnp.exp(score)
                total = jnp.sum(expo, -1, keepdims=True)
                mixed = jnp.dot(
                    expo.astype(jnp.bfloat16), values[:, cols], preferred_element_type=jnp.float32
                )
                outs.append(mixed * (step / total))
            abuf[when, pl.ds(pl.multiple_of(tile * TILE, TILE), TILE), :] = jnp.concatenate(
                outs, axis=1
            )
            return carry

        lax.fori_loop(0, 4, one, 0, unroll=4)

    keys_values(0)
    keys_values(1)
    keys_values(2)
    h_arrive(2)
    norm(3)
    keys_values(3)
    wlast.shared()
    project(0, 2, 3)
    project(1, 2, 3)
    project(2, 2, 3)
    project(3, 2, 3)
    oring.collect(1)
    oring.collect(2)
    oring.collect(3)
    oring.swap()
    attend(0)
    attend(1)
    attend(2)
    attend(3)

    total = abuf[0]
    for k in range(1, 2 * XG):
        total = total + abuf[k]
    tsend[...] = total.astype(jnp.bfloat16)
    push(tsend, trecv, ts, tr, 0, lower)
    remote(trecv, trecv, ts, tr, 0, lower).wait_recv()
    run = jnp.where(yl > 0, trecv[...].astype(jnp.float32), 0.0)
    for k in range(2 * XG):
        sbuf[k] = run.astype(jnp.bfloat16)
        if k < 2 * XG - 1:
            run = run + abuf[k]

    def columns_of(src):
        return sall.at[:, :, pl.ds(pl.multiple_of(src * CW, HD), CW)]

    for k in (1, 3, 2):
        push(sbuf.at[pl.ds(2 * lax.rem(x + k, XG), 2)], columns_of(x), ss, sr, k - 1, at_x(k))
    keep = pltpu.make_async_copy(sbuf.at[pl.ds(2 * x, 2)], columns_of(x), lsem.at[4])
    keep.start()
    oring.swapped()
    oring.shared()
    keep.wait()

    def s_arrive(k):
        source = columns_of(lax.rem(x + XG - k, XG))
        remote(source, source, ss, sr, k - 1, at_x(k)).wait_recv()

    chunk = 256

    def finish(near):
        def one(i, carry):
            column = pl.ds(pl.multiple_of(i * chunk, chunk), chunk)
            before = 0.0
            for k in (0, 1, 3) if near else (2,):
                src = lax.rem(x + k, XG)
                left = sall[:, :, pl.ds(pl.multiple_of(src * CW, HD), CW)].reshape(rows, CW)
                part = pl.ds(lax.rem(src, 2) * (ZG // 2), ZG // 2)
                right = wo[lax.div(src, 2), part, :, :, column].reshape(CW, chunk)
                before = before + jnp.dot(left, right, preferred_element_type=jnp.float32)
            for half in range(2):
                done = before[half * part_rows : (half + 1) * part_rows]
                if near:
                    first = start_ref[:, column].astype(jnp.float32)
                else:
                    first = out_ref[half, :, column]
                out_ref[half, :, column] = first - done
            return carry

        lax.fori_loop(0, width // chunk, one, 0)

    s_arrive(1)
    s_arrive(3)
    finish(True)
    s_arrive(2)
    finish(False)
    wfirst.finish()
    wlast.finish()
    oring.finish()
    copies = [halo(group, j) for group in range(4) for j in range(2)]

    @pl.when(tok < ntok - 1)
    def _():
        for ahead, _ in copies:
            ahead.wait_send()

    @pl.when(tok > 0)
    def _():
        for _, behind in copies:
            behind.wait_send()

    for copy in sent:
        copy.wait_send()


def body(start, trajectory, plan, neighbors, mod_weight, w_qkv, w_out):
    steps_here, tok_here, width = trajectory.shape
    rows = steps_here * tok_here
    half = mod_weight.shape[0] // 2
    freqs = jnp.exp(-math.log(10000.0) * jnp.arange(half, dtype=jnp.float32) / half)[None]
    bf, f32 = jnp.bfloat16, jnp.float32
    kv = pltpu.VMEM((6, 3, steps_here, TILE, CW), bf)
    dma = pltpu.SemaphoreType.DMA
    vmem = pl.BlockSpec(memory_space=pltpu.VMEM)
    smem = pl.BlockSpec(memory_space=pltpu.SMEM)
    hbm = pl.BlockSpec(memory_space=pltpu.HBM)
    return pl.pallas_call(
        kernel,
        out_shape=pltpu.VMEM((steps_here, tok_here, width), f32),
        in_specs=[hbm, smem, vmem, hbm, hbm, hbm, hbm, smem],
        out_specs=vmem,
        scratch_shapes=[
            pltpu.VMEM((tok_here, width), bf),
            pltpu.VMEM((steps_here, tok_here, width), bf),
            pltpu.VMEM(mod_weight.shape, bf),
            pltpu.VMEM((2 * XG, 2 * width), f32),
            pltpu.VMEM((3, rows, width), bf),
            pltpu.VMEM((4, rows, width), bf),
            pltpu.VMEM((2, ZG, 2, w_qkv.shape[0], 3 * CW), bf),
            pltpu.VMEM((2, ZG, 2, w_out.shape[0], width), bf),
            kv, kv, kv, kv,
            pltpu.VMEM((2 * XG, tok_here, CW), f32),
            pltpu.VMEM((tok_here, CW), bf),
            pltpu.VMEM((tok_here, CW), bf),
            pltpu.VMEM((2 * XG, tok_here, CW), bf),
            pltpu.VMEM((steps_here, tok_here, width), bf),
            dma((8,)),
            dma((6,)), dma((6,)),
            dma((62,)), dma((62,)),
            dma((21,)), dma((21,)),
            dma((16,)), dma((16,)),
            dma((1,)), dma((1,)),
            dma((3,)), dma((3,)),
        ],
        compiler_params=pltpu.CompilerParams(
            collective_id=0, has_side_effects=True, vmem_limit_bytes=56 << 20
        ),
    )(trajectory, plan, freqs, mod_weight, w_qkv, w_out, start, neighbors)


def solution(mesh):
    return jax.shard_map(
        body,
        mesh=mesh,
        in_specs=(
            P("tok", None),
            P("tm", "tok", None),
            P(),
            P("tok", None),
            P(),
            P("tok", None),
            P("tok", None),
        ),
        out_specs=P("tm", "tok", None),
        check_vma=False,
    )
```

```python
import math

import jax
import jax.numpy as jnp
from jax import lax
from jax.experimental import pallas as pl
from jax.experimental.pallas import tpu as pltpu
from jax.sharding import PartitionSpec as P

NSCHED = 1000
XG = 4
ZG = 8
HL = 3
HD = 128
CW = HL * HD
TILE = 64
MESH = pl.DeviceIdType.MESH


class Ring:
    eager = True

    def __init__(self, buf, cols, send, recv, base, pos, peers):
        self.buf, self.cols = buf, cols
        self.send, self.recv, self.base = send, recv, base
        self.yl, self.yh, self.z, self.c = pos
        self.peers = peers
        self.sent = []

    def block(self, yh, off, full=False, other=False):
        ref = self.buf.at[yh, lax.rem(self.z + off, ZG), 1 - self.c if other else self.c]
        return ref if full else ref.at[:, self.cols]

    def slot(self, k, yl):
        return yl * (0, 2, 6, 4)[k] + (1 - yl) * (1, 7, 3, 5)[k]

    def copy(self, ref, i, peer):
        i = self.base + i
        return pltpu.make_async_remote_copy(
            src_ref=ref, dst_ref=ref, send_sem=self.send.at[i], recv_sem=self.recv.at[i],
            device_id=self.peers[peer], device_id_type=MESH,
        )

    def push(self, ref, i, peer):
        copy = self.copy(ref, i, peer)
        copy.start()
        self.sent.append(copy)

    def arrive(self, ref, i, peer):
        self.copy(ref, i, peer).wait_recv()

    def give(self, yh, off, i):
        self.push(self.block(yh, off), i, "core")

    def own(self):
        mine = self.block(self.yh, 0)
        self.push(mine, 0, "z+")
        self.push(mine, 4, "z-")
        self.give(self.yh, 0, 15)

    def step(self, s):
        low = self.block(self.yh, ZG - s)
        self.arrive(low, s - 1, "z+")
        if s < 4:
            self.push(low, s, "z+")
            high = self.block(self.yh, s)
            self.arrive(high, 3 + s, "z-")
            if s < 3:
                self.push(high, 4 + s, "z-")
        if self.eager:
            self.push(self.block(self.yh, self.slot(s - 1, self.yl)), 6 + s, "part")
        self.give(self.yh, ZG - s, 15 + ZG - s)
        if s < 4:
            self.give(self.yh, s, 15 + s)

    def relay(self, k):
        off = self.slot(k, 1 - self.yl)
        self.arrive(self.block(1 - self.yh, off), 7 + k, "part")
        self.push(self.block(1 - self.yh, off), 11 + k, "low")
        self.give(1 - self.yh, off, 23 + k)

    def collect(self, k):
        off = self.slot(k, self.yl)
        self.arrive(self.block(1 - self.yh, off), 11 + k, "low")
        self.give(1 - self.yh, off, 27 + k)

    def shared(self):
        for off in range(ZG):
            self.arrive(self.block(self.yh, off, other=True), 15 + off, "core")
        for k in range(4):
            for i, yl in ((23, 1 - self.yl), (27, self.yl)):
                off = self.slot(k, yl)
                self.arrive(self.block(1 - self.yh, off, other=True), i + k, "core")

    def finish(self):
        for copy in self.sent:
            copy.wait_send()


class WideRing(Ring):
    eager = False

    def part(self, k):
        self.push(self.block(self.yh, self.slot(k, self.yl)), 7 + k, "part")

    def give(self, yh, off, i):
        pass

    def whole(self, yh, k, other=False):
        quarter = pl.ds(pl.multiple_of(lax.rem(self.x + k, XG) * self.span, HD), self.span)
        return self.buf.at[yh, :, 1 - self.c if other else self.c, :, quarter]

    def swap(self):
        for yh in range(2):
            self.push(self.whole(yh, 0), 15 + yh, "x+")
            self.push(self.whole(1 - yh, 0), 18 - yh, "x-")
            self.push(self.whole(yh, 0), 21 + yh, "core")

    def forward(self):
        self.arrive(self.whole(0, 3), 15, "x+")
        self.push(self.whole(0, 3), 19, "x+")
        self.push(self.whole(0, 3), 23, "core")
        self.arrive(self.whole(1, 1), 18, "x-")
        self.push(self.whole(1, 1), 20, "x-")
        self.push(self.whole(1, 1), 26, "core")

    def swapped(self):
        self.arrive(self.whole(1, 3), 16, "x+")
        self.push(self.whole(1, 3), 24, "core")
        self.arrive(self.whole(0, 1), 17, "x-")
        self.push(self.whole(0, 1), 25, "core")
        self.arrive(self.whole(0, 2), 19, "x+")
        self.push(self.whole(0, 2), 27, "core")
        self.arrive(self.whole(1, 2), 20, "x-")
        self.push(self.whole(1, 2), 28, "core")

    def shared(self):
        for i, k in ((21, 0), (23, 3), (25, 1), (27, 2)):
            for yh in range(2):
                self.arrive(self.whole(yh, k, True), i + yh, "core")


def kernel(
    x_ref, plan_ref, freq_ref, mod_ref, wqkv_ref, wout_ref, start_hbm, nb_ref, out_ref,
    start_ref, own, modw, mods, hbuf, hnorm, wbuf, wo, kv0, kv1, kv2, kv3, abuf, tsend, trecv, sbuf, pass_on, sall,
    lsem, hs, hr, ws, wr, os, orecv, ks, kr, ts, tr, ss, sr,
):
    tm, tok = lax.axis_index("tm"), lax.axis_index("tok")
    x, yl = lax.rem(tm, XG), lax.div(tm, XG)
    yh, z, c = lax.div(tok, 2 * ZG), lax.div(lax.rem(tok, 2 * ZG), 2), lax.rem(tok, 2)
    part_rows, width = x_ref.shape[1:]
    rows = 2 * part_rows
    ntok = 4 * ZG

    def at_x(k):
        return {"tm": yl * XG + lax.rem(x + k, XG), "tok": tok}

    def at_tok(k):
        return {"tm": tm, "tok": lax.rem(tok + ntok + k, ntok)}

    peers = {
        "z+": {"tm": tm, "tok": yh * 2 * ZG + lax.rem(z + 1, ZG) * 2 + c},
        "z-": {"tm": tm, "tok": yh * 2 * ZG + lax.rem(z + ZG - 1, ZG) * 2 + c},
        "core": {"tm": tm, "tok": yh * 2 * ZG + z * 2 + 1 - c},
        "part": {"tm": (1 - yl) * XG + x, "tok": (1 - yh) * 2 * ZG + z * 2 + c},
        "low": {"tm": (1 - yl) * XG + x, "tok": tok},
        "x+": at_x(1),
        "x-": at_x(3),
    }
    lower = peers["low"]
    beside = at_tok(2 * c - 1)

    own_copies = []
    for j in range(3):
        column = pl.multiple_of(j * width + x * CW, HD)
        own_copies.append(pltpu.make_async_copy(
            wqkv_ref.at[:, pl.ds(column, CW)],
            wbuf.at[yh, z, c, :, pl.ds((j + 2) % 3 * CW, CW)], lsem.at[j],
        ))
    own_copies.append(pltpu.make_async_copy(wout_ref, wo.at[yh, z, c], lsem.at[3]))
    state_copies = [
        pltpu.make_async_copy(x_ref, own, lsem.at[5]),
        pltpu.make_async_copy(mod_ref, modw, lsem.at[6]),
        pltpu.make_async_copy(start_hbm, start_ref, lsem.at[7]),
    ]
    for copy in own_copies + state_copies:
        copy.start()

    barrier = pltpu.get_barrier_semaphore()
    everyone = [at_x(2), *peers.values(), beside]
    for peer in everyone:
        pl.semaphore_signal(barrier, inc=1, device_id=peer, device_id_type=MESH)
    pl.semaphore_wait(barrier, len(everyone))

    sent = []

    def remote(src, dst, s, r, i, peer):
        return pltpu.make_async_remote_copy(
            src_ref=src, dst_ref=dst, send_sem=s.at[i], recv_sem=r.at[i],
            device_id=peer, device_id_type=MESH,
        )

    def push(*args):
        copy = remote(*args)
        copy.start()
        sent.append(copy)

    top, bottom = pl.ds(0, part_rows), pl.ds(part_rows, part_rows)

    push(x_ref.at[0], hbuf.at[0, top], hs, hr, 0, at_x(1))
    push(x_ref.at[1], hbuf.at[0, bottom], hs, hr, 1, at_x(3))
    for copy in own_copies:
        copy.wait()
    pos = (yl, yh, z, c)
    cut = 2 * CW
    wfirst = Ring(wbuf, pl.ds(0, cut), ws, wr, 0, pos, peers)
    wlast = Ring(wbuf, pl.ds(cut, 3 * CW - cut), ws, wr, 31, pos, peers)
    span = width // XG
    oring = WideRing(wo, pl.ds(pl.multiple_of(x * span, HD), span), os, orecv, 0, pos, peers)
    oring.x, oring.span = x, span
    wfirst.own()
    wlast.own()
    oring.own()
    push(x_ref.at[1], hbuf.at[1, top], hs, hr, 2, at_x(1))
    push(x_ref.at[0], hbuf.at[1, bottom], hs, hr, 3, at_x(3))

    def h_arrive(group):
        i = 2 * group
        remote(hbuf.at[group, top], hbuf.at[group, top], hs, hr, i, at_x(1)).wait_recv()
        remote(hbuf.at[group, bottom], hbuf.at[group, bottom], hs, hr, i + 1, at_x(3)).wait_recv()

    def timestep(group, half):
        if group == 0:
            return 2 * x + half
        if group == 3:
            return 2 * lax.rem(x + 2, XG) + half
        owner = lax.rem(x + 3 + 2 * half, XG)
        return 2 * owner + (half if group == 1 else 1 - half)

    def plan_row(k, shape):
        return jnp.full(shape, plan_ref[yl * 2 * XG + k].astype(jnp.float32)) / NSCHED

    def time_of(k):
        return plan_row(k, (1, HD))

    def modulation():
        times = jnp.concatenate([plan_row(k, (1, freq_ref.shape[1])) for k in range(2 * XG)], axis=0)
        angle = 1000.0 * times * freq_ref[...]
        embed = jnp.concatenate([jnp.cos(angle), jnp.sin(angle)], axis=1)
        act = (embed / (1.0 + jnp.exp(-embed))).astype(jnp.bfloat16)
        mods[...] = jnp.dot(act, modw[...], preferred_element_type=jnp.float32)

    band = 16

    def norm(group):
        def one(i, carry):
            half, row = lax.div(i, part_rows // band), lax.rem(i, part_rows // band) * band
            at = pl.ds(pl.multiple_of(row, band), band)
            if group == 0:
                values = own[half, at, :]
            else:
                at_row = pl.multiple_of(i * band, band)
                values = hbuf[group - 1, pl.ds(at_row, band), :]
            values = values.astype(jnp.float32)
            when = timestep(group, half)
            shift = mods[pl.ds(when, 1), :width]
            scale = mods[pl.ds(when, 1), width:]
            center = values - jnp.mean(values, -1, keepdims=True)
            spread = jnp.mean(center * center, -1, keepdims=True)
            done = center * lax.rsqrt(spread + 1e-06) * (1.0 + scale) + shift
            hnorm[group, pl.ds(pl.multiple_of(i * band, band), band), :] = done.astype(jnp.bfloat16)
            return carry

        lax.fori_loop(0, rows // band, one, 0, unroll=4)

    for copy in state_copies:
        copy.wait()
    modulation()
    norm(0)
    wfirst.step(1)
    wlast.step(1)
    oring.step(1)
    oring.part(0)
    wfirst.step(2)
    wlast.step(2)
    wfirst.relay(0)
    wlast.relay(0)
    oring.step(2)
    oring.part(1)
    wfirst.step(3)
    wlast.step(3)
    h_arrive(0)
    push(hbuf.at[0, top], hbuf.at[2, top], hs, hr, 4, at_x(1))
    push(hbuf.at[0, bottom], hbuf.at[2, bottom], hs, hr, 5, at_x(3))
    norm(1)
    wfirst.relay(1)
    wlast.relay(1)
    wfirst.collect(0)
    wlast.collect(0)
    oring.step(3)
    oring.part(2)
    oring.relay(0)
    wfirst.step(4)
    wlast.step(4)
    wfirst.relay(2)
    wlast.relay(2)
    wfirst.collect(1)
    wlast.collect(1)
    oring.step(4)
    oring.part(3)
    oring.relay(1)
    wfirst.relay(3)
    wlast.relay(3)
    oring.relay(2)
    h_arrive(1)
    norm(2)
    wfirst.collect(2)
    wlast.collect(2)
    oring.collect(0)
    wfirst.collect(3)
    wlast.collect(3)
    oring.relay(3)
    wfirst.shared()

    kvs = (kv0, kv1, kv2, kv3)

    def project(group, first, last):
        kv = kvs[group]

        def one(j, carry):
            column = pl.multiple_of(j * CW, HD)
            left = hnorm[group]
            right = wbuf[:, :, :, :, pl.ds(column, CW)].reshape(width, CW)
            part = jnp.dot(left, right, preferred_element_type=jnp.float32)
            pieces = []
            for head in range(HL):
                piece = part[:, head * HD : (head + 1) * HD]
                norm = lax.rsqrt(jnp.mean(piece * piece, -1, keepdims=True) + 1e-06)
                pieces.append(piece * jnp.where(j == 1, 1.0, norm))
            done = jnp.concatenate(pieces, axis=1).astype(jnp.bfloat16)
            for half in range(2):
                for tile in range(2):
                    row = half * part_rows + tile * TILE
                    kv[2 + tile, j, half] = done[row : row + TILE]
            return carry

        lax.fori_loop(first, last, one, 0)

    def halo(group, j):
        mine = kvs[group].at[2:4, j]
        i = 4 * group + 2 * j
        return (
            remote(mine, kvs[group].at[0:2, j], ks, kr, i, at_tok(1)),
            remote(mine, kvs[group].at[4:6, j], ks, kr, i + 1, at_tok(-1)),
        )

    def keys_values(group):
        for j in range(2):
            project(group, j, j + 1)
            ahead, behind = halo(group, j)

            @pl.when(tok < ntok - 1)
            def _():
                ahead.start()

            @pl.when(tok > 0)
            def _():
                behind.start()

    def attend(group):
        kv = kvs[group]
        copies = [halo(group, j) for j in range(2)]

        @pl.when(tok > 0)
        def _():
            for ahead, _ in copies:
                ahead.wait_recv()

        @pl.when(tok < ntok - 1)
        def _():
            for _, behind in copies:
                behind.wait_recv()


        def one(i, carry):
            half, tile = lax.div(i, 2), lax.rem(i, 2)
            when = timestep(group, half)
            step = time_of(when) - time_of(when + 1)
            near = [
                jnp.clip(nb_ref[tile, n] - (2 * tok - 2), 0, 5) for n in range(nb_ref.shape[1])
            ]
            query = kv[2 + tile, 2, half]
            keys = jnp.concatenate([kv[n, 0, half] for n in near], axis=0)
            values = jnp.concatenate([kv[n, 1, half] for n in near], axis=0)
            outs = []
            for head in range(HL):
                cols = slice(head * HD, (head + 1) * HD)
                score = lax.dot_general(
                    query[:, cols], keys[:, cols], (((1,), (1,)), ((), ())),
                    preferred_element_type=jnp.float32,
                ) * (1.0 / math.sqrt(HD))
                expo = jnp.exp(score)
                total = jnp.sum(expo, -1, keepdims=True)
                mixed = jnp.dot(
                    expo.astype(jnp.bfloat16), values[:, cols], preferred_element_type=jnp.float32
                )
                outs.append(mixed * (step / total))
            abuf[when, pl.ds(pl.multiple_of(tile * TILE, TILE), TILE), :] = jnp.concatenate(
                outs, axis=1
            )
            return carry

        lax.fori_loop(0, 4, one, 0, unroll=4)

    keys_values(0)
    keys_values(1)
    oring.collect(1)
    oring.collect(2)
    oring.collect(3)
    oring.swap()
    keys_values(2)
    h_arrive(2)
    norm(3)
    keys_values(3)
    wlast.shared()
    project(0, 2, 3)
    project(1, 2, 3)
    project(2, 2, 3)
    project(3, 2, 3)
    attend(0)
    oring.forward()
    attend(1)
    attend(2)
    attend(3)

    total = abuf[0]
    for k in range(1, 2 * XG):
        total = total + abuf[k]
    tsend[...] = total.astype(jnp.bfloat16)
    push(tsend, trecv, ts, tr, 0, lower)
    oring.swapped()
    remote(trecv, trecv, ts, tr, 0, lower).wait_recv()
    run = jnp.where(yl > 0, trecv[...].astype(jnp.float32), 0.0)
    for k in range(2 * XG):
        sbuf[k] = run.astype(jnp.bfloat16)
        if k < 2 * XG - 1:
            run = run + abuf[k]

    def columns_of(src):
        return sall.at[:, :, pl.ds(pl.multiple_of(src * CW, HD), CW)]

    def piece(half, src):
        return sall.at[half, :, pl.ds(pl.multiple_of(src * CW, HD), CW)]

    far = lax.rem(x + 2, XG)
    for half, k in ((0, 1), (1, 3)):
        push(sbuf.at[2 * far + half], pass_on.at[half], ss, sr, 2 + half, at_x(k))
    for k in (1, 3):
        push(sbuf.at[pl.ds(2 * lax.rem(x + k, XG), 2)], columns_of(x), ss, sr, k // 2, at_x(k))
    for half, k in ((0, 1), (1, 3)):
        remote(pass_on.at[half], pass_on.at[half], ss, sr, 2 + half, at_x(k)).wait_recv()
        push(
            pass_on.at[half], piece(half, lax.rem(x + XG - k, XG)), ss, sr, 4 + half, at_x(k)
        )
    keep = pltpu.make_async_copy(sbuf.at[pl.ds(2 * x, 2)], columns_of(x), lsem.at[4])
    keep.start()
    oring.shared()
    keep.wait()

    def s_arrive(k):
        if k == 2:
            for half, via in ((0, 1), (1, 3)):
                source = piece(half, far)
                remote(source, source, ss, sr, 4 + half, at_x(via)).wait_recv()
        else:
            source = columns_of(lax.rem(x + XG - k, XG))
            remote(source, source, ss, sr, k // 2, at_x(k)).wait_recv()

    chunk = 256

    def finish(near):
        def one(i, carry):
            column = pl.ds(pl.multiple_of(i * chunk, chunk), chunk)
            before = 0.0
            for k in (0, 1, 3) if near else (2,):
                src = lax.rem(x + k, XG)
                left = sall[:, :, pl.ds(pl.multiple_of(src * CW, HD), CW)].reshape(rows, CW)
                part = pl.ds(lax.rem(src, 2) * (ZG // 2), ZG // 2)
                right = wo[lax.div(src, 2), part, :, :, column].reshape(CW, chunk)
                before = before + jnp.dot(left, right, preferred_element_type=jnp.float32)
            for half in range(2):
                done = before[half * part_rows : (half + 1) * part_rows]
                if near:
                    first = start_ref[:, column].astype(jnp.float32)
                else:
                    first = out_ref[half, :, column]
                out_ref[half, :, column] = first - done
            return carry

        lax.fori_loop(0, width // chunk, one, 0)

    s_arrive(1)
    s_arrive(3)
    finish(True)
    s_arrive(2)
    finish(False)
    wfirst.finish()
    wlast.finish()
    oring.finish()
    copies = [halo(group, j) for group in range(4) for j in range(2)]

    @pl.when(tok < ntok - 1)
    def _():
        for ahead, _ in copies:
            ahead.wait_send()

    @pl.when(tok > 0)
    def _():
        for _, behind in copies:
            behind.wait_send()

    for copy in sent:
        copy.wait_send()


def body(start, trajectory, plan, neighbors, mod_weight, w_qkv, w_out):
    steps_here, tok_here, width = trajectory.shape
    rows = steps_here * tok_here
    half = mod_weight.shape[0] // 2
    freqs = jnp.exp(-math.log(10000.0) * jnp.arange(half, dtype=jnp.float32) / half)[None]
    bf, f32 = jnp.bfloat16, jnp.float32
    kv = pltpu.VMEM((6, 3, steps_here, TILE, CW), bf)
    dma = pltpu.SemaphoreType.DMA
    vmem = pl.BlockSpec(memory_space=pltpu.VMEM)
    smem = pl.BlockSpec(memory_space=pltpu.SMEM)
    hbm = pl.BlockSpec(memory_space=pltpu.HBM)
    return pl.pallas_call(
        kernel,
        out_shape=pltpu.VMEM((steps_here, tok_here, width), f32),
        in_specs=[hbm, smem, vmem, hbm, hbm, hbm, hbm, smem],
        out_specs=vmem,
        scratch_shapes=[
            pltpu.VMEM((tok_here, width), bf),
            pltpu.VMEM((steps_here, tok_here, width), bf),
            pltpu.VMEM(mod_weight.shape, bf),
            pltpu.VMEM((2 * XG, 2 * width), f32),
            pltpu.VMEM((3, rows, width), bf),
            pltpu.VMEM((4, rows, width), bf),
            pltpu.VMEM((2, ZG, 2, w_qkv.shape[0], 3 * CW), bf),
            pltpu.VMEM((2, ZG, 2, w_out.shape[0], width), bf),
            kv, kv, kv, kv,
            pltpu.VMEM((2 * XG, tok_here, CW), f32),
            pltpu.VMEM((tok_here, CW), bf),
            pltpu.VMEM((tok_here, CW), bf),
            pltpu.VMEM((2 * XG, tok_here, CW), bf),
            pltpu.VMEM((2, tok_here, CW), bf),
            pltpu.VMEM((steps_here, tok_here, width), bf),
            dma((8,)),
            dma((6,)), dma((6,)),
            dma((62,)), dma((62,)),
            dma((29,)), dma((29,)),
            dma((16,)), dma((16,)),
            dma((1,)), dma((1,)),
            dma((6,)), dma((6,)),
        ],
        compiler_params=pltpu.CompilerParams(
            collective_id=0, has_side_effects=True, vmem_limit_bytes=56 << 20
        ),
    )(trajectory, plan, freqs, mod_weight, w_qkv, w_out, start, neighbors)


def solution(mesh):
    return jax.shard_map(
        body,
        mesh=mesh,
        in_specs=(
            P("tok", None),
            P("tm", "tok", None),
            P(),
            P("tok", None),
            P(),
            P("tok", None),
            P("tok", None),
        ),
        out_specs=P("tm", "tok", None),
        check_vma=False,
    )
```

```python
import math

import jax
import jax.numpy as jnp
from jax import lax
from jax.experimental import pallas as pl
from jax.experimental.pallas import tpu as pltpu
from jax.sharding import PartitionSpec as P

NSCHED = 1000
XG = 4
ZG = 8
HL = 3
HD = 128
CW = HL * HD
TILE = 64
MESH = pl.DeviceIdType.MESH


class Ring:
    eager = True

    def __init__(self, buf, cols, send, recv, base, pos, peers):
        self.buf, self.cols = buf, cols
        self.send, self.recv, self.base = send, recv, base
        self.yl, self.yh, self.z, self.c = pos
        self.peers = peers
        self.sent = []

    def block(self, yh, off, full=False, other=False):
        ref = self.buf.at[yh, lax.rem(self.z + off, ZG), 1 - self.c if other else self.c]
        return ref if full else ref.at[:, self.cols]

    def slot(self, k, yl):
        return yl * (0, 2, 6, 4)[k] + (1 - yl) * (1, 7, 3, 5)[k]

    def copy(self, ref, i, peer):
        i = self.base + i
        return pltpu.make_async_remote_copy(
            src_ref=ref, dst_ref=ref, send_sem=self.send.at[i], recv_sem=self.recv.at[i],
            device_id=self.peers[peer], device_id_type=MESH,
        )

    def push(self, ref, i, peer):
        copy = self.copy(ref, i, peer)
        copy.start()
        self.sent.append(copy)

    def arrive(self, ref, i, peer):
        self.copy(ref, i, peer).wait_recv()

    def give(self, yh, off, i):
        self.push(self.block(yh, off), i, "core")

    def own(self):
        mine = self.block(self.yh, 0)
        self.push(mine, 0, "z+")
        self.push(mine, 4, "z-")
        self.give(self.yh, 0, 15)

    def step(self, s):
        low = self.block(self.yh, ZG - s)
        self.arrive(low, s - 1, "z+")
        if s < 4:
            self.push(low, s, "z+")
            high = self.block(self.yh, s)
            self.arrive(high, 3 + s, "z-")
            if s < 3:
                self.push(high, 4 + s, "z-")
        if self.eager:
            self.push(self.block(self.yh, self.slot(s - 1, self.yl)), 6 + s, "part")
        self.give(self.yh, ZG - s, 15 + ZG - s)
        if s < 4:
            self.give(self.yh, s, 15 + s)

    def relay(self, k):
        off = self.slot(k, 1 - self.yl)
        self.arrive(self.block(1 - self.yh, off), 7 + k, "part")
        self.push(self.block(1 - self.yh, off), 11 + k, "low")
        self.give(1 - self.yh, off, 23 + k)

    def collect(self, k):
        off = self.slot(k, self.yl)
        self.arrive(self.block(1 - self.yh, off), 11 + k, "low")
        self.give(1 - self.yh, off, 27 + k)

    def shared(self):
        for off in range(ZG):
            self.arrive(self.block(self.yh, off, other=True), 15 + off, "core")
        for k in range(4):
            for i, yl in ((23, 1 - self.yl), (27, self.yl)):
                off = self.slot(k, yl)
                self.arrive(self.block(1 - self.yh, off, other=True), i + k, "core")

    def finish(self):
        for copy in self.sent:
            copy.wait_send()


class WideRing(Ring):
    eager = False

    def part(self, k):
        self.push(self.block(self.yh, self.slot(k, self.yl)), 7 + k, "part")

    def give(self, yh, off, i):
        pass

    def whole(self, yh, k, other=False):
        quarter = pl.ds(pl.multiple_of(lax.rem(self.x + k, XG) * self.span, HD), self.span)
        return self.buf.at[yh, :, 1 - self.c if other else self.c, :, quarter]

    def swap(self):
        for yh in range(2):
            self.push(self.whole(yh, 0), 15 + yh, "x+")
            self.push(self.whole(1 - yh, 0), 18 - yh, "x-")
            self.push(self.whole(yh, 0), 21 + yh, "core")

    def forward(self):
        self.arrive(self.whole(0, 3), 15, "x+")
        self.push(self.whole(0, 3), 19, "x+")
        self.push(self.whole(0, 3), 23, "core")
        self.arrive(self.whole(1, 1), 18, "x-")
        self.push(self.whole(1, 1), 20, "x-")
        self.push(self.whole(1, 1), 26, "core")

    def swapped(self):
        self.arrive(self.whole(1, 3), 16, "x+")
        self.push(self.whole(1, 3), 24, "core")
        self.arrive(self.whole(0, 1), 17, "x-")
        self.push(self.whole(0, 1), 25, "core")
        self.arrive(self.whole(0, 2), 19, "x+")
        self.push(self.whole(0, 2), 27, "core")
        self.arrive(self.whole(1, 2), 20, "x-")
        self.push(self.whole(1, 2), 28, "core")

    def shared(self):
        for i, k in ((21, 0), (23, 3), (25, 1), (27, 2)):
            for yh in range(2):
                self.arrive(self.whole(yh, k, True), i + yh, "core")


def kernel(
    x_ref, plan_ref, freq_ref, mod_ref, wqkv_ref, wout_ref, start_hbm, nb_ref, out_ref,
    start_ref, probs, gains, own, modw, mods, hbuf, hnorm, wbuf, wo, qs, k0, k1, k2, k3, v0, v1, v2, v3, abuf, tsend, trecv, sbuf, pass_on, sall,
    lsem, hs, hr, ws, wr, os, orecv, ks, kr, ts, tr, ss, sr,
):
    tm, tok = lax.axis_index("tm"), lax.axis_index("tok")
    x, yl = lax.rem(tm, XG), lax.div(tm, XG)
    yh, z, c = lax.div(tok, 2 * ZG), lax.div(lax.rem(tok, 2 * ZG), 2), lax.rem(tok, 2)
    part_rows, width = x_ref.shape[1:]
    rows = 2 * part_rows
    ntok = 4 * ZG

    def at_x(k):
        return {"tm": yl * XG + lax.rem(x + k, XG), "tok": tok}

    def at_tok(k):
        return {"tm": tm, "tok": lax.rem(tok + ntok + k, ntok)}

    peers = {
        "z+": {"tm": tm, "tok": yh * 2 * ZG + lax.rem(z + 1, ZG) * 2 + c},
        "z-": {"tm": tm, "tok": yh * 2 * ZG + lax.rem(z + ZG - 1, ZG) * 2 + c},
        "core": {"tm": tm, "tok": yh * 2 * ZG + z * 2 + 1 - c},
        "part": {"tm": (1 - yl) * XG + x, "tok": (1 - yh) * 2 * ZG + z * 2 + c},
        "low": {"tm": (1 - yl) * XG + x, "tok": tok},
        "x+": at_x(1),
        "x-": at_x(3),
    }
    lower = peers["low"]
    beside = at_tok(2 * c - 1)

    own_copies = []
    for j in range(3):
        column = pl.multiple_of(j * width + x * CW, HD)
        own_copies.append(pltpu.make_async_copy(
            wqkv_ref.at[:, pl.ds(column, CW)],
            wbuf.at[yh, z, c, :, pl.ds((j + 2) % 3 * CW, CW)], lsem.at[j],
        ))
    own_copies.append(pltpu.make_async_copy(wout_ref, wo.at[yh, z, c], lsem.at[3]))
    state_copies = [
        pltpu.make_async_copy(x_ref, own, lsem.at[5]),
        pltpu.make_async_copy(mod_ref, modw, lsem.at[6]),
        pltpu.make_async_copy(start_hbm, start_ref, lsem.at[7]),
    ]
    for copy in own_copies + state_copies:
        copy.start()

    barrier = pltpu.get_barrier_semaphore()
    everyone = [at_x(2), *peers.values(), beside]
    for peer in everyone:
        pl.semaphore_signal(barrier, inc=1, device_id=peer, device_id_type=MESH)
    pl.semaphore_wait(barrier, len(everyone))

    sent = []

    def remote(src, dst, s, r, i, peer):
        return pltpu.make_async_remote_copy(
            src_ref=src, dst_ref=dst, send_sem=s.at[i], recv_sem=r.at[i],
            device_id=peer, device_id_type=MESH,
        )

    def push(*args):
        copy = remote(*args)
        copy.start()
        sent.append(copy)

    top, bottom = pl.ds(0, part_rows), pl.ds(part_rows, part_rows)

    push(x_ref.at[0], hbuf.at[0, top], hs, hr, 0, at_x(1))
    push(x_ref.at[1], hbuf.at[0, bottom], hs, hr, 1, at_x(3))
    for copy in own_copies:
        copy.wait()
    pos = (yl, yh, z, c)
    cut = 2 * CW
    wfirst = Ring(wbuf, pl.ds(0, cut), ws, wr, 0, pos, peers)
    wlast = Ring(wbuf, pl.ds(cut, 3 * CW - cut), ws, wr, 31, pos, peers)
    span = width // XG
    oring = WideRing(wo, pl.ds(pl.multiple_of(x * span, HD), span), os, orecv, 0, pos, peers)
    oring.x, oring.span = x, span
    wfirst.own()
    wlast.own()
    oring.own()
    push(x_ref.at[1], hbuf.at[1, top], hs, hr, 2, at_x(1))
    push(x_ref.at[0], hbuf.at[1, bottom], hs, hr, 3, at_x(3))

    def h_arrive(group):
        i = 2 * group
        remote(hbuf.at[group, top], hbuf.at[group, top], hs, hr, i, at_x(1)).wait_recv()
        remote(hbuf.at[group, bottom], hbuf.at[group, bottom], hs, hr, i + 1, at_x(3)).wait_recv()

    def timestep(group, half):
        if group == 0:
            return 2 * x + half
        if group == 3:
            return 2 * lax.rem(x + 2, XG) + half
        owner = lax.rem(x + 3 + 2 * half, XG)
        return 2 * owner + (half if group == 1 else 1 - half)

    def plan_row(k, shape):
        return jnp.full(shape, plan_ref[yl * 2 * XG + k].astype(jnp.float32)) / NSCHED

    def time_of(k):
        return plan_row(k, (1, HD))

    def modulation():
        times = jnp.concatenate([plan_row(k, (1, freq_ref.shape[1])) for k in range(2 * XG)], axis=0)
        angle = 1000.0 * times * freq_ref[...]
        embed = jnp.concatenate([jnp.cos(angle), jnp.sin(angle)], axis=1)
        act = (embed / (1.0 + jnp.exp(-embed))).astype(jnp.bfloat16)
        mods[...] = jnp.dot(act, modw[...], preferred_element_type=jnp.float32)

    band = 16

    def norm(group):
        def one(i, carry):
            half, row = lax.div(i, part_rows // band), lax.rem(i, part_rows // band) * band
            at = pl.ds(pl.multiple_of(row, band), band)
            if group == 0:
                values = own[half, at, :]
            else:
                at_row = pl.multiple_of(i * band, band)
                values = hbuf[group - 1, pl.ds(at_row, band), :]
            values = values.astype(jnp.float32)
            when = timestep(group, half)
            shift = mods[pl.ds(when, 1), :width]
            scale = mods[pl.ds(when, 1), width:]
            center = values - jnp.mean(values, -1, keepdims=True)
            spread = jnp.mean(center * center, -1, keepdims=True)
            done = center * lax.rsqrt(spread + 1e-06) * (1.0 + scale) + shift
            hnorm[group, pl.ds(pl.multiple_of(i * band, band), band), :] = done.astype(jnp.bfloat16)
            return carry

        lax.fori_loop(0, rows // band, one, 0, unroll=4)

    for copy in state_copies:
        copy.wait()
    modulation()
    norm(0)
    wfirst.step(1)
    wlast.step(1)
    oring.step(1)
    oring.part(0)
    wfirst.step(2)
    wlast.step(2)
    wfirst.relay(0)
    wlast.relay(0)
    oring.step(2)
    oring.part(1)
    wfirst.step(3)
    wlast.step(3)
    h_arrive(0)
    push(hbuf.at[0, top], hbuf.at[2, top], hs, hr, 4, at_x(1))
    push(hbuf.at[0, bottom], hbuf.at[2, bottom], hs, hr, 5, at_x(3))
    norm(1)
    wfirst.relay(1)
    wlast.relay(1)
    wfirst.collect(0)
    wlast.collect(0)
    oring.step(3)
    oring.part(2)
    oring.relay(0)
    wfirst.step(4)
    wlast.step(4)
    wfirst.relay(2)
    wlast.relay(2)
    wfirst.collect(1)
    wlast.collect(1)
    oring.step(4)
    oring.part(3)
    oring.relay(1)
    wfirst.relay(3)
    wlast.relay(3)
    oring.relay(2)
    h_arrive(1)
    norm(2)
    wfirst.collect(2)
    wlast.collect(2)
    oring.collect(0)
    wfirst.collect(3)
    wlast.collect(3)
    oring.relay(3)
    wfirst.shared()

    ks_of, vs_of = (k0, k1, k2, k3), (v0, v1, v2, v3)

    def project(group, j):
        left = hnorm[group]
        right = wbuf[:, :, :, :, j * CW : (j + 1) * CW].reshape(width, CW)
        part = jnp.dot(left, right, preferred_element_type=jnp.float32)
        pieces = []
        for head in range(HL):
            piece = part[:, head * HD : (head + 1) * HD]
            if j != 1:
                piece = piece * lax.rsqrt(jnp.mean(piece * piece, -1, keepdims=True) + 1e-06)
            pieces.append(piece)
        done = jnp.concatenate(pieces, axis=1).astype(jnp.bfloat16)
        for half in range(2):
            for tile in range(2):
                row = half * part_rows + tile * TILE
                piece = done[row : row + TILE]
                if j == 2:
                    qs[group, tile, half] = piece
                else:
                    (ks_of, vs_of)[j][group][2 + tile, half] = piece

    def halo(group, j):
        ref = (ks_of, vs_of)[j][group]
        mine = ref.at[2:4]
        i = 4 * group + 2 * j
        return (
            remote(mine, ref.at[0:2], ks, kr, i, at_tok(1)),
            remote(mine, ref.at[4:6], ks, kr, i + 1, at_tok(-1)),
        )

    def keys_values(group):
        for j in range(2):
            project(group, j)
            ahead, behind = halo(group, j)

            @pl.when(tok < ntok - 1)
            def _():
                ahead.start()

            @pl.when(tok > 0)
            def _():
                behind.start()

    def attend(group):
        copies = [halo(group, j) for j in range(2)]

        def arrived(j):
            @pl.when(tok > 0)
            def _():
                copies[j][0].wait_recv()

            @pl.when(tok < ntok - 1)
            def _():
                copies[j][1].wait_recv()

        def near(tile):
            return [
                jnp.clip(nb_ref[tile, n] - (2 * tok - 2), 0, 5) for n in range(nb_ref.shape[1])
            ]

        def weigh(i, carry):
            half, tile = lax.div(i, 2), lax.rem(i, 2)
            when = timestep(group, half)
            step = time_of(when) - time_of(when + 1)
            query = qs[group, tile, half]
            keys = jnp.concatenate([ks_of[group][n, half] for n in near(tile)], axis=0)
            for head in range(HL):
                cols = slice(head * HD, (head + 1) * HD)
                score = lax.dot_general(
                    query[:, cols], keys[:, cols], (((1,), (1,)), ((), ())),
                    preferred_element_type=jnp.float32,
                ) * (1.0 / math.sqrt(HD))
                expo = jnp.exp(score)
                total = jnp.sum(expo, -1, keepdims=True)
                probs[i, head] = expo.astype(jnp.bfloat16)
                gains[i, head] = step / total
            return carry

        def mix(i, carry):
            half, tile = lax.div(i, 2), lax.rem(i, 2)
            values = jnp.concatenate([vs_of[group][n, half] for n in near(tile)], axis=0)
            outs = []
            for head in range(HL):
                mixed = jnp.dot(
                    probs[i, head], values[:, head * HD : (head + 1) * HD],
                    preferred_element_type=jnp.float32,
                )
                outs.append(mixed * gains[i, head])
            rows_at = pl.ds(pl.multiple_of(tile * TILE, TILE), TILE)
            abuf[timestep(group, half), rows_at, :] = jnp.concatenate(outs, axis=1)
            return carry

        arrived(0)
        lax.fori_loop(0, 4, weigh, 0, unroll=4)
        arrived(1)
        lax.fori_loop(0, 4, mix, 0, unroll=4)

    keys_values(0)
    keys_values(1)
    oring.collect(1)
    oring.collect(2)
    oring.collect(3)
    oring.swap()
    keys_values(2)
    h_arrive(2)
    norm(3)
    keys_values(3)
    wlast.shared()
    project(0, 2)
    project(1, 2)
    project(2, 2)
    project(3, 2)
    attend(0)
    attend(1)
    oring.forward()
    attend(2)
    attend(3)

    total = abuf[0]
    for k in range(1, 2 * XG):
        total = total + abuf[k]
    tsend[...] = total.astype(jnp.bfloat16)
    push(tsend, trecv, ts, tr, 0, lower)
    remote(trecv, trecv, ts, tr, 0, lower).wait_recv()
    run = jnp.where(yl > 0, trecv[...].astype(jnp.float32), 0.0)
    for k in range(2 * XG):
        sbuf[k] = run.astype(jnp.bfloat16)
        if k < 2 * XG - 1:
            run = run + abuf[k]

    def columns_of(src):
        return sall.at[:, :, pl.ds(pl.multiple_of(src * CW, HD), CW)]

    def piece(half, src):
        return sall.at[half, :, pl.ds(pl.multiple_of(src * CW, HD), CW)]

    far = lax.rem(x + 2, XG)
    for half, k in ((0, 1), (1, 3)):
        push(sbuf.at[2 * far + half], pass_on.at[half], ss, sr, 2 + half, at_x(k))
    for k in (1, 3):
        push(sbuf.at[pl.ds(2 * lax.rem(x + k, XG), 2)], columns_of(x), ss, sr, k // 2, at_x(k))
    oring.swapped()
    for half, k in ((0, 1), (1, 3)):
        remote(pass_on.at[half], pass_on.at[half], ss, sr, 2 + half, at_x(k)).wait_recv()
        push(
            pass_on.at[half], piece(half, lax.rem(x + XG - k, XG)), ss, sr, 4 + half, at_x(k)
        )
    keep = pltpu.make_async_copy(sbuf.at[pl.ds(2 * x, 2)], columns_of(x), lsem.at[4])
    keep.start()
    oring.shared()
    keep.wait()

    def s_arrive(k):
        if k == 2:
            for half, via in ((0, 1), (1, 3)):
                source = piece(half, far)
                remote(source, source, ss, sr, 4 + half, at_x(via)).wait_recv()
        else:
            source = columns_of(lax.rem(x + XG - k, XG))
            remote(source, source, ss, sr, k // 2, at_x(k)).wait_recv()

    chunk = 256

    def finish(near):
        def one(i, carry):
            column = pl.ds(pl.multiple_of(i * chunk, chunk), chunk)
            before = 0.0
            for k in (0, 1, 3) if near else (2,):
                src = lax.rem(x + k, XG)
                left = sall[:, :, pl.ds(pl.multiple_of(src * CW, HD), CW)].reshape(rows, CW)
                part = pl.ds(lax.rem(src, 2) * (ZG // 2), ZG // 2)
                right = wo[lax.div(src, 2), part, :, :, column].reshape(CW, chunk)
                before = before + jnp.dot(left, right, preferred_element_type=jnp.float32)
            for half in range(2):
                done = before[half * part_rows : (half + 1) * part_rows]
                if near:
                    first = start_ref[:, column].astype(jnp.float32)
                else:
                    first = out_ref[half, :, column]
                out_ref[half, :, column] = first - done
            return carry

        lax.fori_loop(0, width // chunk, one, 0)

    s_arrive(1)
    s_arrive(3)
    finish(True)
    s_arrive(2)
    finish(False)
    wfirst.finish()
    wlast.finish()
    oring.finish()
    copies = [halo(group, j) for group in range(4) for j in range(2)]

    @pl.when(tok < ntok - 1)
    def _():
        for ahead, _ in copies:
            ahead.wait_send()

    @pl.when(tok > 0)
    def _():
        for _, behind in copies:
            behind.wait_send()

    for copy in sent:
        copy.wait_send()


def body(start, trajectory, plan, neighbors, mod_weight, w_qkv, w_out):
    steps_here, tok_here, width = trajectory.shape
    rows = steps_here * tok_here
    half = mod_weight.shape[0] // 2
    freqs = jnp.exp(-math.log(10000.0) * jnp.arange(half, dtype=jnp.float32) / half)[None]
    bf, f32 = jnp.bfloat16, jnp.float32
    kv = pltpu.VMEM((6, steps_here, TILE, CW), bf)
    dma = pltpu.SemaphoreType.DMA
    vmem = pl.BlockSpec(memory_space=pltpu.VMEM)
    smem = pl.BlockSpec(memory_space=pltpu.SMEM)
    hbm = pl.BlockSpec(memory_space=pltpu.HBM)
    return pl.pallas_call(
        kernel,
        out_shape=pltpu.VMEM((steps_here, tok_here, width), f32),
        in_specs=[hbm, smem, vmem, hbm, hbm, hbm, hbm, smem],
        out_specs=vmem,
        scratch_shapes=[
            pltpu.VMEM((tok_here, width), bf),
            pltpu.VMEM((4, HL, TILE, 3 * TILE), bf),
            pltpu.VMEM((4, HL, TILE, HD), f32),
            pltpu.VMEM((steps_here, tok_here, width), bf),
            pltpu.VMEM(mod_weight.shape, bf),
            pltpu.VMEM((2 * XG, 2 * width), f32),
            pltpu.VMEM((3, rows, width), bf),
            pltpu.VMEM((4, rows, width), bf),
            pltpu.VMEM((2, ZG, 2, w_qkv.shape[0], 3 * CW), bf),
            pltpu.VMEM((2, ZG, 2, w_out.shape[0], width), bf),
            pltpu.VMEM((4, 2, steps_here, TILE, CW), bf),
            kv, kv, kv, kv, kv, kv, kv, kv,
            pltpu.VMEM((2 * XG, tok_here, CW), f32),
            pltpu.VMEM((tok_here, CW), bf),
            pltpu.VMEM((tok_here, CW), bf),
            pltpu.VMEM((2 * XG, tok_here, CW), bf),
            pltpu.VMEM((2, tok_here, CW), bf),
            pltpu.VMEM((steps_here, tok_here, width), bf),
            dma((8,)),
            dma((6,)), dma((6,)),
            dma((62,)), dma((62,)),
            dma((29,)), dma((29,)),
            dma((16,)), dma((16,)),
            dma((1,)), dma((1,)),
            dma((6,)), dma((6,)),
        ],
        compiler_params=pltpu.CompilerParams(
            collective_id=0, has_side_effects=True, vmem_limit_bytes=56 << 20
        ),
    )(trajectory, plan, freqs, mod_weight, w_qkv, w_out, start, neighbors)


def solution(mesh):
    return jax.shard_map(
        body,
        mesh=mesh,
        in_specs=(
            P("tok", None),
            P("tm", "tok", None),
            P(),
            P("tok", None),
            P(),
            P("tok", None),
            P("tok", None),
        ),
        out_specs=P("tm", "tok", None),
        check_vma=False,
    )
```

```python
import math

import jax
import jax.numpy as jnp
from jax import lax
from jax.experimental import pallas as pl
from jax.experimental.pallas import tpu as pltpu
from jax.sharding import PartitionSpec as P

NSCHED = 1000
XG = 4
ZG = 8
HL = 3
HD = 128
CW = HL * HD
TILE = 64
MESH = pl.DeviceIdType.MESH


class Ring:
    eager = True

    def __init__(self, buf, cols, send, recv, base, pos, peers):
        self.buf, self.cols = buf, cols
        self.send, self.recv, self.base = send, recv, base
        self.yl, self.yh, self.z, self.c = pos
        self.peers = peers
        self.sent = []

    def block(self, yh, off, full=False, other=False):
        ref = self.buf.at[yh, lax.rem(self.z + off, ZG), 1 - self.c if other else self.c]
        return ref if full else ref.at[:, self.cols]

    def slot(self, k, yl):
        return yl * (0, 2, 6, 4)[k] + (1 - yl) * (1, 7, 3, 5)[k]

    def copy(self, ref, i, peer):
        i = self.base + i
        return pltpu.make_async_remote_copy(
            src_ref=ref, dst_ref=ref, send_sem=self.send.at[i], recv_sem=self.recv.at[i],
            device_id=self.peers[peer], device_id_type=MESH,
        )

    def push(self, ref, i, peer):
        copy = self.copy(ref, i, peer)
        copy.start()
        self.sent.append(copy)

    def arrive(self, ref, i, peer):
        self.copy(ref, i, peer).wait_recv()

    def give(self, yh, off, i):
        self.push(self.block(yh, off), i, "core")

    def own(self):
        mine = self.block(self.yh, 0)
        self.push(mine, 0, "z+")
        self.push(mine, 4, "z-")
        self.give(self.yh, 0, 15)

    def step(self, s):
        low = self.block(self.yh, ZG - s)
        self.arrive(low, s - 1, "z+")
        if s < 4:
            self.push(low, s, "z+")
            high = self.block(self.yh, s)
            self.arrive(high, 3 + s, "z-")
            if s < 3:
                self.push(high, 4 + s, "z-")
        if self.eager:
            self.push(self.block(self.yh, self.slot(s - 1, self.yl)), 6 + s, "part")
        self.give(self.yh, ZG - s, 15 + ZG - s)
        if s < 4:
            self.give(self.yh, s, 15 + s)

    def relay(self, k):
        off = self.slot(k, 1 - self.yl)
        self.arrive(self.block(1 - self.yh, off), 7 + k, "part")
        self.push(self.block(1 - self.yh, off), 11 + k, "low")
        self.give(1 - self.yh, off, 23 + k)

    def collect(self, k):
        off = self.slot(k, self.yl)
        self.arrive(self.block(1 - self.yh, off), 11 + k, "low")
        self.give(1 - self.yh, off, 27 + k)

    def shared(self):
        for off in range(ZG):
            self.arrive(self.block(self.yh, off, other=True), 15 + off, "core")
        for k in range(4):
            for i, yl in ((23, 1 - self.yl), (27, self.yl)):
                off = self.slot(k, yl)
                self.arrive(self.block(1 - self.yh, off, other=True), i + k, "core")

    def finish(self):
        for copy in self.sent:
            copy.wait_send()


class WideRing(Ring):
    eager = False

    def part(self, k):
        self.push(self.block(self.yh, self.slot(k, self.yl)), 7 + k, "part")

    def give(self, yh, off, i):
        pass

    def whole(self, yh, k, other=False):
        quarter = pl.ds(pl.multiple_of(lax.rem(self.x + k, XG) * self.span, HD), self.span)
        return self.buf.at[yh, :, 1 - self.c if other else self.c, :, quarter]

    def swap(self):
        for yh in range(2):
            self.push(self.whole(yh, 0), 15 + yh, "x+")
            self.push(self.whole(1 - yh, 0), 18 - yh, "x-")
            self.push(self.whole(yh, 0), 21 + yh, "core")

    def forward(self):
        self.arrive(self.whole(0, 3), 15, "x+")
        self.push(self.whole(0, 3), 19, "x+")
        self.push(self.whole(0, 3), 23, "core")
        self.arrive(self.whole(1, 1), 18, "x-")
        self.push(self.whole(1, 1), 20, "x-")
        self.push(self.whole(1, 1), 26, "core")

    def swapped(self):
        self.arrive(self.whole(1, 3), 16, "x+")
        self.push(self.whole(1, 3), 24, "core")
        self.arrive(self.whole(0, 1), 17, "x-")
        self.push(self.whole(0, 1), 25, "core")
        self.arrive(self.whole(0, 2), 19, "x+")
        self.push(self.whole(0, 2), 27, "core")
        self.arrive(self.whole(1, 2), 20, "x-")
        self.push(self.whole(1, 2), 28, "core")

    def shared(self):
        for i, k in ((21, 0), (23, 3), (25, 1), (27, 2)):
            for yh in range(2):
                self.arrive(self.whole(yh, k, True), i + yh, "core")


def kernel(
    x_ref, plan_ref, freq_ref, mod_ref, wqkv_ref, wout_ref, start_hbm, nb_ref, out_ref,
    start_ref, probs, gains, own, modw, mods, hbuf, hnorm, wbuf, wo, qs, k0, k1, k2, k3, v0, v1, v2, v3, abuf, tsend, trecv, sbuf, pass_on, sall,
    lsem, hs, hr, ws, wr, os, orecv, ks, kr, ts, tr, ss, sr,
):
    tm, tok = lax.axis_index("tm"), lax.axis_index("tok")
    x, yl = lax.rem(tm, XG), lax.div(tm, XG)
    yh, z, c = lax.div(tok, 2 * ZG), lax.div(lax.rem(tok, 2 * ZG), 2), lax.rem(tok, 2)
    part_rows, width = x_ref.shape[1:]
    rows = 2 * part_rows
    ntok = 4 * ZG

    def at_x(k):
        return {"tm": yl * XG + lax.rem(x + k, XG), "tok": tok}

    def at_tok(k):
        return {"tm": tm, "tok": lax.rem(tok + ntok + k, ntok)}

    peers = {
        "z+": {"tm": tm, "tok": yh * 2 * ZG + lax.rem(z + 1, ZG) * 2 + c},
        "z-": {"tm": tm, "tok": yh * 2 * ZG + lax.rem(z + ZG - 1, ZG) * 2 + c},
        "core": {"tm": tm, "tok": yh * 2 * ZG + z * 2 + 1 - c},
        "part": {"tm": (1 - yl) * XG + x, "tok": (1 - yh) * 2 * ZG + z * 2 + c},
        "low": {"tm": (1 - yl) * XG + x, "tok": tok},
        "x+": at_x(1),
        "x-": at_x(3),
    }
    lower = peers["low"]
    beside = at_tok(2 * c - 1)

    own_copies = []
    for j in range(3):
        column = pl.multiple_of(j * width + x * CW, HD)
        own_copies.append(pltpu.make_async_copy(
            wqkv_ref.at[:, pl.ds(column, CW)],
            wbuf.at[yh, z, c, :, pl.ds((j + 2) % 3 * CW, CW)], lsem.at[j],
        ))
    own_copies.append(pltpu.make_async_copy(wout_ref, wo.at[yh, z, c], lsem.at[3]))
    state_copies = [
        pltpu.make_async_copy(x_ref, own, lsem.at[5]),
        pltpu.make_async_copy(mod_ref, modw, lsem.at[6]),
        pltpu.make_async_copy(start_hbm, start_ref, lsem.at[7]),
    ]
    for copy in own_copies + state_copies:
        copy.start()

    barrier = pltpu.get_barrier_semaphore()
    everyone = [at_x(2), *peers.values(), beside]
    for peer in everyone:
        pl.semaphore_signal(barrier, inc=1, device_id=peer, device_id_type=MESH)
    pl.semaphore_wait(barrier, len(everyone))

    sent = []

    def remote(src, dst, s, r, i, peer):
        return pltpu.make_async_remote_copy(
            src_ref=src, dst_ref=dst, send_sem=s.at[i], recv_sem=r.at[i],
            device_id=peer, device_id_type=MESH,
        )

    def push(*args):
        copy = remote(*args)
        copy.start()
        sent.append(copy)

    top, bottom = pl.ds(0, part_rows), pl.ds(part_rows, part_rows)

    push(x_ref.at[0], hbuf.at[0, top], hs, hr, 0, at_x(1))
    push(x_ref.at[1], hbuf.at[0, bottom], hs, hr, 1, at_x(3))
    for copy in own_copies:
        copy.wait()
    pos = (yl, yh, z, c)
    cut = 2 * CW
    wfirst = Ring(wbuf, pl.ds(0, cut), ws, wr, 0, pos, peers)
    wlast = Ring(wbuf, pl.ds(cut, 3 * CW - cut), ws, wr, 31, pos, peers)
    span = width // XG
    oring = WideRing(wo, pl.ds(pl.multiple_of(x * span, HD), span), os, orecv, 0, pos, peers)
    oring.x, oring.span = x, span
    wfirst.own()
    wlast.own()
    oring.own()
    push(x_ref.at[1], hbuf.at[1, top], hs, hr, 2, at_x(1))
    push(x_ref.at[0], hbuf.at[1, bottom], hs, hr, 3, at_x(3))

    def h_arrive(group):
        i = 2 * group
        remote(hbuf.at[group, top], hbuf.at[group, top], hs, hr, i, at_x(1)).wait_recv()
        remote(hbuf.at[group, bottom], hbuf.at[group, bottom], hs, hr, i + 1, at_x(3)).wait_recv()

    def timestep(group, half):
        if group == 0:
            return 2 * x + half
        if group == 3:
            return 2 * lax.rem(x + 2, XG) + half
        owner = lax.rem(x + 3 + 2 * half, XG)
        return 2 * owner + (half if group == 1 else 1 - half)

    def plan_row(k, shape):
        return jnp.full(shape, plan_ref[yl * 2 * XG + k].astype(jnp.float32)) / NSCHED

    def time_of(k):
        return plan_row(k, (1, HD))

    def modulation():
        times = jnp.concatenate([plan_row(k, (1, freq_ref.shape[1])) for k in range(2 * XG)], axis=0)
        angle = 1000.0 * times * freq_ref[...]
        embed = jnp.concatenate([jnp.cos(angle), jnp.sin(angle)], axis=1)
        act = (embed / (1.0 + jnp.exp(-embed))).astype(jnp.bfloat16)
        mods[...] = jnp.dot(act, modw[...], preferred_element_type=jnp.float32)

    band = 16

    def norm(group):
        def one(i, carry):
            half, row = lax.div(i, part_rows // band), lax.rem(i, part_rows // band) * band
            at = pl.ds(pl.multiple_of(row, band), band)
            if group == 0:
                values = own[half, at, :]
            else:
                at_row = pl.multiple_of(i * band, band)
                values = hbuf[group - 1, pl.ds(at_row, band), :]
            values = values.astype(jnp.float32)
            when = timestep(group, half)
            shift = mods[pl.ds(when, 1), :width]
            scale = mods[pl.ds(when, 1), width:]
            center = values - jnp.mean(values, -1, keepdims=True)
            spread = jnp.mean(center * center, -1, keepdims=True)
            done = center * lax.rsqrt(spread + 1e-06) * (1.0 + scale) + shift
            hnorm[group, pl.ds(pl.multiple_of(i * band, band), band), :] = done.astype(jnp.bfloat16)
            return carry

        lax.fori_loop(0, rows // band, one, 0, unroll=4)

    for copy in state_copies:
        copy.wait()
    modulation()
    norm(0)
    wfirst.step(1)
    wlast.step(1)
    oring.step(1)
    oring.part(0)
    wfirst.step(2)
    wlast.step(2)
    wfirst.relay(0)
    wlast.relay(0)
    oring.step(2)
    oring.part(1)
    wfirst.step(3)
    wlast.step(3)
    h_arrive(0)
    push(hbuf.at[0, top], hbuf.at[2, top], hs, hr, 4, at_x(1))
    push(hbuf.at[0, bottom], hbuf.at[2, bottom], hs, hr, 5, at_x(3))
    norm(1)
    wfirst.relay(1)
    wlast.relay(1)
    wfirst.collect(0)
    wlast.collect(0)
    oring.step(3)
    oring.part(2)
    oring.relay(0)
    wfirst.step(4)
    wlast.step(4)
    wfirst.relay(2)
    wlast.relay(2)
    wfirst.collect(1)
    wlast.collect(1)
    oring.step(4)
    oring.part(3)
    oring.relay(1)
    wfirst.relay(3)
    wlast.relay(3)
    oring.relay(2)
    h_arrive(1)
    norm(2)
    wfirst.collect(2)
    wlast.collect(2)
    oring.collect(0)
    wfirst.collect(3)
    wlast.collect(3)
    oring.relay(3)
    wfirst.shared()

    ks_of, vs_of = (k0, k1, k2, k3), (v0, v1, v2, v3)

    def project(group, j):
        left = hnorm[group]
        right = wbuf[:, :, :, :, j * CW : (j + 1) * CW].reshape(width, CW)
        part = jnp.dot(left, right, preferred_element_type=jnp.float32)
        pieces = []
        for head in range(HL):
            piece = part[:, head * HD : (head + 1) * HD]
            if j != 1:
                piece = piece * lax.rsqrt(jnp.mean(piece * piece, -1, keepdims=True) + 1e-06)
            pieces.append(piece)
        done = jnp.concatenate(pieces, axis=1).astype(jnp.bfloat16)
        for half in range(2):
            for tile in range(2):
                row = half * part_rows + tile * TILE
                piece = done[row : row + TILE]
                if j == 2:
                    qs[group, tile, half] = piece
                else:
                    (ks_of, vs_of)[j][group][2 + tile, half] = piece

    def halo(group, j):
        ref = (ks_of, vs_of)[j][group]
        mine = ref.at[2:4]
        i = 4 * group + 2 * j
        return (
            remote(mine, ref.at[0:2], ks, kr, i, at_tok(1)),
            remote(mine, ref.at[4:6], ks, kr, i + 1, at_tok(-1)),
        )

    def keys_values(group):
        for j in range(2):
            project(group, j)
            ahead, behind = halo(group, j)

            @pl.when(tok < ntok - 1)
            def _():
                ahead.start()

            @pl.when(tok > 0)
            def _():
                behind.start()

    def attend(group):
        copies = [halo(group, j) for j in range(2)]

        def arrived(j):
            @pl.when(tok > 0)
            def _():
                copies[j][0].wait_recv()

            @pl.when(tok < ntok - 1)
            def _():
                copies[j][1].wait_recv()

        def near(tile):
            return [
                jnp.clip(nb_ref[tile, n] - (2 * tok - 2), 0, 5) for n in range(nb_ref.shape[1])
            ]

        def weigh(i, carry):
            half, tile = lax.div(i, 2), lax.rem(i, 2)
            when = timestep(group, half)
            step = time_of(when) - time_of(when + 1)
            query = qs[group, tile, half]
            keys = jnp.concatenate([ks_of[group][n, half] for n in near(tile)], axis=0)
            for head in range(HL):
                cols = slice(head * HD, (head + 1) * HD)
                score = lax.dot_general(
                    query[:, cols], keys[:, cols], (((1,), (1,)), ((), ())),
                    preferred_element_type=jnp.float32,
                ) * (1.0 / math.sqrt(HD))
                expo = jnp.exp(score)
                total = jnp.sum(expo, -1, keepdims=True)
                probs[i, head] = expo.astype(jnp.bfloat16)
                gains[i, head] = step / total
            return carry

        def mix(i, carry):
            half, tile = lax.div(i, 2), lax.rem(i, 2)
            values = jnp.concatenate([vs_of[group][n, half] for n in near(tile)], axis=0)
            outs = []
            for head in range(HL):
                mixed = jnp.dot(
                    probs[i, head], values[:, head * HD : (head + 1) * HD],
                    preferred_element_type=jnp.float32,
                )
                outs.append(mixed * gains[i, head])
            rows_at = pl.ds(pl.multiple_of(tile * TILE, TILE), TILE)
            abuf[timestep(group, half), rows_at, :] = jnp.concatenate(outs, axis=1)
            return carry

        arrived(0)
        lax.fori_loop(0, 4, weigh, 0, unroll=4)
        arrived(1)
        lax.fori_loop(0, 4, mix, 0, unroll=4)

    keys_values(0)
    keys_values(1)
    oring.collect(1)
    oring.collect(2)
    oring.collect(3)
    oring.swap()
    keys_values(2)
    h_arrive(2)
    norm(3)
    keys_values(3)
    wlast.shared()
    project(0, 2)
    project(1, 2)
    project(2, 2)
    project(3, 2)
    attend(0)
    attend(1)
    oring.forward()
    attend(2)
    attend(3)

    total = abuf[0]
    for k in range(1, 2 * XG):
        total = total + abuf[k]
    tsend[...] = total.astype(jnp.bfloat16)
    push(tsend, trecv, ts, tr, 0, lower)
    remote(trecv, trecv, ts, tr, 0, lower).wait_recv()
    run = jnp.where(yl > 0, trecv[...].astype(jnp.float32), 0.0)
    for k in range(2 * XG):
        sbuf[k] = run.astype(jnp.bfloat16)
        if k < 2 * XG - 1:
            run = run + abuf[k]

    def columns_of(src):
        return sall.at[:, :, pl.ds(pl.multiple_of(src * CW, HD), CW)]

    def piece(half, src):
        return sall.at[half, :, pl.ds(pl.multiple_of(src * CW, HD), CW)]

    far = lax.rem(x + 2, XG)
    for half, k in ((0, 1), (1, 3)):
        push(sbuf.at[2 * far + half], pass_on.at[half], ss, sr, 2 + half, at_x(k))
    for k in (1, 3):
        push(sbuf.at[pl.ds(2 * lax.rem(x + k, XG), 2)], columns_of(x), ss, sr, k // 2, at_x(k))
    oring.swapped()
    for half, k in ((0, 1), (1, 3)):
        remote(pass_on.at[half], pass_on.at[half], ss, sr, 2 + half, at_x(k)).wait_recv()
        push(
            pass_on.at[half], piece(half, lax.rem(x + XG - k, XG)), ss, sr, 4 + half, at_x(k)
        )
    keep = pltpu.make_async_copy(sbuf.at[pl.ds(2 * x, 2)], columns_of(x), lsem.at[4])
    keep.start()
    oring.shared()
    keep.wait()

    def s_arrive(k):
        if k == 2:
            for half, via in ((0, 1), (1, 3)):
                source = piece(half, far)
                remote(source, source, ss, sr, 4 + half, at_x(via)).wait_recv()
        else:
            source = columns_of(lax.rem(x + XG - k, XG))
            remote(source, source, ss, sr, k // 2, at_x(k)).wait_recv()

    chunk = 256

    def finish(hops):
        def one(i, carry):
            column = pl.ds(pl.multiple_of(i * chunk, chunk), chunk)
            before = 0.0
            for k in hops:
                src = lax.rem(x + k, XG)
                left = sall[:, :, pl.ds(pl.multiple_of(src * CW, HD), CW)].reshape(rows, CW)
                part = pl.ds(lax.rem(src, 2) * (ZG // 2), ZG // 2)
                right = wo[lax.div(src, 2), part, :, :, column].reshape(CW, chunk)
                before = before + jnp.dot(left, right, preferred_element_type=jnp.float32)
            for half in range(2):
                done = before[half * part_rows : (half + 1) * part_rows]
                if 0 in hops:
                    first = start_ref[:, column].astype(jnp.float32)
                else:
                    first = out_ref[half, :, column]
                out_ref[half, :, column] = first - done
            return carry

        lax.fori_loop(0, width // chunk, one, 0, unroll=2)

    finish((0,))
    s_arrive(1)
    s_arrive(3)
    finish((1, 3))
    s_arrive(2)
    finish((2,))
    wfirst.finish()
    wlast.finish()
    oring.finish()
    copies = [halo(group, j) for group in range(4) for j in range(2)]

    @pl.when(tok < ntok - 1)
    def _():
        for ahead, _ in copies:
            ahead.wait_send()

    @pl.when(tok > 0)
    def _():
        for _, behind in copies:
            behind.wait_send()

    for copy in sent:
        copy.wait_send()


def body(start, trajectory, plan, neighbors, mod_weight, w_qkv, w_out):
    steps_here, tok_here, width = trajectory.shape
    rows = steps_here * tok_here
    half = mod_weight.shape[0] // 2
    freqs = jnp.exp(-math.log(10000.0) * jnp.arange(half, dtype=jnp.float32) / half)[None]
    bf, f32 = jnp.bfloat16, jnp.float32
    kv = pltpu.VMEM((6, steps_here, TILE, CW), bf)
    dma = pltpu.SemaphoreType.DMA
    vmem = pl.BlockSpec(memory_space=pltpu.VMEM)
    smem = pl.BlockSpec(memory_space=pltpu.SMEM)
    hbm = pl.BlockSpec(memory_space=pltpu.HBM)
    return pl.pallas_call(
        kernel,
        out_shape=pltpu.VMEM((steps_here, tok_here, width), f32),
        in_specs=[hbm, smem, vmem, hbm, hbm, hbm, hbm, smem],
        out_specs=vmem,
        scratch_shapes=[
            pltpu.VMEM((tok_here, width), bf),
            pltpu.VMEM((4, HL, TILE, 3 * TILE), bf),
            pltpu.VMEM((4, HL, TILE, HD), f32),
            pltpu.VMEM((steps_here, tok_here, width), bf),
            pltpu.VMEM(mod_weight.shape, bf),
            pltpu.VMEM((2 * XG, 2 * width), f32),
            pltpu.VMEM((3, rows, width), bf),
            pltpu.VMEM((4, rows, width), bf),
            pltpu.VMEM((2, ZG, 2, w_qkv.shape[0], 3 * CW), bf),
            pltpu.VMEM((2, ZG, 2, w_out.shape[0], width), bf),
            pltpu.VMEM((4, 2, steps_here, TILE, CW), bf),
            kv, kv, kv, kv, kv, kv, kv, kv,
            pltpu.VMEM((2 * XG, tok_here, CW), f32),
            pltpu.VMEM((tok_here, CW), bf),
            pltpu.VMEM((tok_here, CW), bf),
            pltpu.VMEM((2 * XG, tok_here, CW), bf),
            pltpu.VMEM((2, tok_here, CW), bf),
            pltpu.VMEM((steps_here, tok_here, width), bf),
            dma((8,)),
            dma((6,)), dma((6,)),
            dma((62,)), dma((62,)),
            dma((29,)), dma((29,)),
            dma((16,)), dma((16,)),
            dma((1,)), dma((1,)),
            dma((6,)), dma((6,)),
        ],
        compiler_params=pltpu.CompilerParams(
            collective_id=0, has_side_effects=True, vmem_limit_bytes=56 << 20
        ),
    )(trajectory, plan, freqs, mod_weight, w_qkv, w_out, start, neighbors)


def solution(mesh):
    return jax.shard_map(
        body,
        mesh=mesh,
        in_specs=(
            P("tok", None),
            P("tm", "tok", None),
            P(),
            P("tok", None),
            P(),
            P("tok", None),
            P("tok", None),
        ),
        out_specs=P("tm", "tok", None),
        check_vma=False,
    )
```
